512 devices in a mesh: gz: 16 (over z, core), xy: 32 (over y, x).
Axes of the slice: x: 4, y: 8, z: 8, core: 2. Of those that a mesh axis runs over, the one named last changes fastest.
Arguments:
- density: float32 [512, 64, 512], P('xy', 'gz'), may hold values from 0.5 to 2
- momentum: float32 [3, 512, 64, 512], P(None, 'xy', 'gz'), may hold values from -3 to 3
- magnetic: float32 [3, 512, 64, 512], P(None, 'xy', 'gz'), may hold values from -3 to 3
- arm_potential: float32 [512, 512], P('xy'), may hold values from -10 to 10
- sn_cells: int32 [512, 3], P(('gz', 'xy')), may hold values from 0 to 511, as said below
- sn_counts: int32 [512], P(('gz', 'xy')), may hold values from 0 to 3
Outputs:
- new_density: float32 [512, 64, 512], P('xy', 'gz')
- new_momentum: float32 [3, 512, 64, 512], P(None, 'xy', 'gz')
- new_magnetic: float32 [3, 512, 64, 512], P(None, 'xy', 'gz')
- density_modes: float32 [2, 64, 512, 512], P(None, 'gz', 'xy')
The draws below stay inside these ranges and needn't reach their ends.
Inputs may be any that keep to these rules, and one draw needn't show every extreme that they name: `sn_cells`: row e is the centre of an event held by device e // 1 of the joined axes gz+xy (gz slowest); its x lies among that device's 16 x rows and its z among its 4 z planes. `sn_counts`: 0 marks an empty slot.
All inputs are finite; a program needn't handle non-finite values.
Results may differ from the reference program's by a relative error of at most 0.00023.
Values sent between devices are 32-bit elements; how exact they have to be, the bound alone decides.
A program may use at most 128 MiB of HBM per device.

```python
import math
import jax
import jax.numpy as jnp
from jax import lax

NX = 512
NY = 512
ZPL = 4
EV_DEV = 1
SUPERNOVA_RADIUS = 16
NZ = 64
XROWS = 16
EVENTS = 512


def draw_sn_cells(key, part):
    slot_ids = jnp.arange(EVENTS, dtype=jnp.int32)
    owner = slot_ids // EV_DEV
    across = NX // XROWS
    tile_row = owner % across
    tile_plane = owner // across
    keys = jax.random.split(key, 3)
    cell_row = tile_row * XROWS + jax.random.randint(keys[0], (EVENTS,), 0, XROWS, dtype=jnp.int32)
    cell_col = jax.random.randint(keys[1], (EVENTS,), 0, NY, dtype=jnp.int32)
    cell_col = jnp.where(slot_ids == 0, 0, cell_col).astype(jnp.int32)
    cell_col = jnp.where(slot_ids == EVENTS - 1, NY - 1, cell_col).astype(jnp.int32)
    cell_plane = tile_plane * ZPL + jax.random.randint(keys[2], (EVENTS,), 0, ZPL, dtype=jnp.int32)
    return jnp.stack([cell_row, cell_col, cell_plane], axis=1)


def set_ends(array, key, least, largest):
    longest = array.shape.index(max(array.shape))
    spots = []
    for shift in (0, 1):
        where = [jax.random.randint(jax.random.fold_in(key, axis), (), 0, length) for axis, length in enumerate(array.shape)]
        where[longest] = (where[longest] + shift) % array.shape[longest]
        spots.append(tuple(where))
    return array.at[spots[0]].set(least).at[spots[1]].set(largest)


def block_levels(key, shape, pieces, least, top_value):
    def one(dim, shards_of):
        heights = jax.random.uniform(jax.random.fold_in(jax.random.fold_in(key, 6), dim), (shards_of,), jnp.float32, least / len(pieces), top_value / len(pieces))
        return jnp.repeat(jnp.exp(heights), shape[dim] // shards_of).reshape((-1,) + (1,) * (len(shape) - dim - 1))

    gain = one(*pieces[0])
    for cut in pieces[1:]:
        gain = gain * one(*cut)
    return gain


def normal_values(own_key, dims, scale, bound, shards=(), kind=jnp.bfloat16):
    factor_of = block_levels(own_key, dims, shards, -0.22, 0.18) if shards else 1.0
    drawn = jax.random.normal(own_key, dims, jnp.float32) * scale * factor_of
    return jnp.minimum(jnp.maximum(drawn, -bound), bound).astype(kind)


def setup_inputs(seed: int = 0) -> dict:
    key_list = jax.random.split(jax.random.key(seed), 7)
    density = jnp.clip(jnp.exp(math.log(2.0) - 1.3862944 * jax.random.uniform(key_list[0], (NX, NZ, NY), jnp.float32) ** block_levels(key_list[0], (NX, NZ, NY), ((0, 32), (1, 16)), -0.2, 0.2)), 0.5, 2.0)
    momentum = normal_values(key_list[1], (3, NX, NZ, NY), 0.5, 3.0, ((1, 32), (2, 16)), jnp.float32)
    magnetic = normal_values(key_list[2], (3, NX, NZ, NY), 0.5, 3.0, ((1, 32), (2, 16)), jnp.float32)
    arm_potential = normal_values(key_list[3], (NX, NY), 2.0, 10.0, ((0, 32),), jnp.float32)
    sn_cells = draw_sn_cells(jax.random.fold_in(key_list[6], 71), 0)
    sn_counts = set_ends(jax.random.randint(key_list[5], (EVENTS,), 0, 4), jax.random.fold_in(key_list[5], 1), 0, 3).astype(jnp.int32)
    return {"density": density, "momentum": momentum, "magnetic": magnetic, "arm_potential": arm_potential, "sn_cells": sn_cells, "sn_counts": sn_counts}


sound_square = 1.0
time_step = 0.1
diffusion = 0.05
mass_yield = 1.0
push_yield = 2.0

def fluxes(mass_density, momenta, induction, direction):
    velocity = [momenta[component] / mass_density for component in range(3)]
    pressure = sound_square * mass_density + 0.5 * (induction[0] * induction[0] + induction[1] * induction[1] + induction[2] * induction[2])
    result = [momenta[direction]]
    for component in range(3):
        term = momenta[component] * velocity[direction] - induction[component] * induction[direction]
        if component == direction:
            term = term + pressure
        result.append(term)
    for component in range(3):
        result.append(velocity[direction] * induction[component] - induction[direction] * velocity[component])
    return result

def central_wrap(field, axis):
    return (jnp.roll(field, 2, axis) - 8.0 * jnp.roll(field, 1, axis) + 8.0 * jnp.roll(field, -1, axis) - jnp.roll(field, -2, axis)) / 12.0

def second_wrap(field, axis):
    return jnp.roll(field, 1, axis) + jnp.roll(field, -1, axis) - 2.0 * field

def reference(density, momentum, magnetic, arm_potential, sn_cells, sn_counts):
    window = jnp.arange(-SUPERNOVA_RADIUS, SUPERNOVA_RADIUS, dtype=jnp.int32)
    radial_distance = window.astype(jnp.float32)
    radius_squared = radial_distance[:, None, None] * radial_distance[:, None, None] + radial_distance[None, :, None] * radial_distance[None, :, None] + radial_distance[None, None, :] * radial_distance[None, None, :]
    blast_profile = jnp.maximum(1.0 - radius_squared / (SUPERNOVA_RADIUS * SUPERNOVA_RADIUS), 0.0)
    impulse = push_yield / SUPERNOVA_RADIUS * blast_profile
    blocks = jnp.stack([mass_yield * blast_profile, impulse * radial_distance[:, None, None], impulse * radial_distance[None, None, :], impulse * radial_distance[None, :, None]])

    def add_event(number, total):
        centre = sn_cells[number]
        row_ids = ((centre[0] + window) % NX).astype(jnp.int32)
        col_ids = ((centre[1] + window) % NY).astype(jnp.int32)
        plane_ids = ((centre[2] + window) % NZ).astype(jnp.int32)
        weighting = sn_counts[number].astype(jnp.float32)
        return total.at[:, row_ids[:, None, None], plane_ids[None, :, None], col_ids[None, None, :]].add(weighting * blocks)
    source = lax.fori_loop(0, sn_counts.shape[0], add_event, jnp.zeros((4, NX, NZ, NY), jnp.float32))
    mass_density = density + source[0]
    momenta = [momentum[component] + source[1 + component] for component in range(3)]
    induction = [magnetic[component] for component in range(3)]
    fields_all = [mass_density] + momenta + induction
    axes = (0, 2, 1)
    updated = list(fields_all)
    for direction in range(3):
        flux_list = fluxes(mass_density, momenta, induction, direction)
        for component in range(7):
            updated[component] = updated[component] - time_step * central_wrap(flux_list[component], axes[direction]) + diffusion * second_wrap(fields_all[component], axes[direction])
    potential = arm_potential[:, None, :]
    updated[1] = updated[1] - time_step * mass_density * central_wrap(potential, 0)
    updated[2] = updated[2] - time_step * mass_density * central_wrap(potential, 2)
    spectrum = jnp.fft.fft2(updated[0], axes=(0, 2)) / math.sqrt(NX * NY)
    stacked = jnp.stack([jnp.real(spectrum), jnp.imag(spectrum)]).astype(jnp.float32)
    stacked = jnp.transpose(stacked, (0, 2, 3, 1))
    stacked = stacked.at[:, :, 0, 0].set(0.0)
    return (updated[0], jnp.stack(updated[1:4]), jnp.stack(updated[4:7]), stacked)
```

```python
import jax
import jax.numpy as jnp
import ml_dtypes
import numpy as np
from jax import lax
from jax.experimental import pallas as pl
from jax.experimental.pallas import tpu as pltpu
from jax.sharding import PartitionSpec as P

MESH = pl.DeviceIdType.MESH
F32 = jnp.float32
BF16 = jnp.bfloat16

NX, NY = 512, 512
XR, ZP = 16, 4
RX, RZ = 5, 11
SLOTS = 64
REACH = 32
A = -0.1 / 12.0
DIFF = 0.05
TILE = (XR + 4) * 8


def tables():
    wave = np.arange(NY)
    angle = (wave[:, None] * wave[None, :] % NY) * (2.0 * np.pi / NY)
    full = np.concatenate([np.cos(angle), np.sin(angle)], axis=1)
    high = full.astype(ml_dtypes.bfloat16)
    low = (full - high.astype(np.float64)).astype(ml_dtypes.bfloat16)
    return high, low


def split(value):
    high = value.astype(BF16)
    return high, (value - high.astype(F32)).astype(BF16)


def ring(flux, field, axis):
    size = flux.shape[axis]
    near = DIFF * field
    steep = (8.0 * A) * flux
    far = A * flux
    return (
        pltpu.roll(near - steep, 1, axis)
        + pltpu.roll(near + steep, size - 1, axis)
        + pltpu.roll(far, 2, axis)
        - pltpu.roll(far, size - 2, axis)
    )


def kernel(
    nxy, ngz,
    rho_ref, mom_ref, mag_ref, pot_ref, cells_ref, counts_ref, hi_ref, lo_ref,
    orho_ref, omom_ref, omag_ref, omode_ref,
    u, src, fx, pot, ev, amat, bmat, hi, lo, nd, nmom, nmag, rmat, outbox, inbox, modes,
    local_sem, evz_s, evz_r, evx_s, evx_r, halo_s, halo_r, a2a_s, a2a_r, out_sem,
):
    me_xy = lax.axis_index("xy")
    me_gz = lax.axis_index("gz")

    def xy(k):
        return lax.rem(me_xy + (k + nxy), nxy)

    def gz(k):
        return lax.rem(me_gz + (k + ngz), ngz)

    local = [
        pltpu.make_async_copy(rho_ref, u.at[0, 2:18, 2:6], local_sem.at[0]),
        pltpu.make_async_copy(mom_ref, u.at[1:4, 2:18, 2:6], local_sem.at[1]),
        pltpu.make_async_copy(mag_ref, u.at[4:7, 2:18, 2:6], local_sem.at[2]),
        pltpu.make_async_copy(pot_ref, pot.at[8:24], local_sem.at[3]),
        pltpu.make_async_copy(hi_ref, hi, local_sem.at[4]),
        pltpu.make_async_copy(lo_ref, lo, local_sem.at[5]),
    ]
    for copy in local:
        copy.start()

    lane = lax.broadcasted_iota(jnp.int32, (1, 128), 1)
    row = jnp.where(lane == 0, cells_ref[0, 0], 0)
    row = jnp.where(lane == 1, cells_ref[0, 1], row)
    row = jnp.where(lane == 2, cells_ref[0, 2], row)
    row = jnp.where(lane == 3, counts_ref[0], row)
    centre = (RX // 2) * RZ
    ev[centre + RZ // 2] = row.astype(F32)
    for slot in range(RX * RZ, SLOTS):
        ev[slot] = jnp.zeros((1, 128), F32)

    barrier = pltpu.get_barrier_semaphore()

    @pl.loop(1, nxy)
    def _(k):
        pl.semaphore_signal(barrier, inc=1, device_id={"xy": xy(k)}, device_id_type=MESH)

    zsteps = [k for k in range(-(RZ // 2), RZ // 2 + 1) if k]
    xsteps = [k for k in range(-(RX // 2), RX // 2 + 1) if k]
    for k in zsteps:
        pl.semaphore_signal(barrier, inc=1, device_id={"gz": gz(k)}, device_id_type=MESH)
    pl.semaphore_wait(barrier, nxy - 1 + len(zsteps))

    def send(source, target, sems, recvs, index, where):
        return pltpu.make_async_remote_copy(
            src_ref=source, dst_ref=target, send_sem=sems.at[index], recv_sem=recvs.at[index],
            device_id=where, device_id_type=MESH,
        )

    evz = []
    for index, k in enumerate(zsteps):
        copy = send(
            ev.at[centre + RZ // 2], ev.at[centre + RZ // 2 - k], evz_s, evz_r, index, {"gz": gz(k)}
        )
        copy.start()
        evz.append(copy)

    up, down = {"xy": xy(1)}, {"xy": xy(-1)}
    above, below = {"gz": gz(1)}, {"gz": gz(-1)}
    low_x, high_x = slice(0, 2), slice(18, 20)
    low_z, high_z = slice(0, 2), slice(6, 8)
    own_x, own_z = slice(2, 18), slice(2, 6)
    pairs = [
        (rho_ref.at[:, 2:4], u.at[0, own_x, low_z], above),
        (rho_ref.at[:, 0:2], u.at[0, own_x, high_z], below),
        (mom_ref.at[2, :, 2:4], u.at[3, own_x, low_z], above),
        (mom_ref.at[2, :, 0:2], u.at[3, own_x, high_z], below),
        (rho_ref.at[14:16], u.at[0, low_x, own_z], up),
        (rho_ref.at[0:2], u.at[0, high_x, own_z], down),
        (mom_ref.at[0, 14:16], u.at[1, low_x, own_z], up),
        (mom_ref.at[0, 0:2], u.at[1, high_x, own_z], down),
        (mom_ref.at[0:2, :, 2:4], u.at[1:3, own_x, low_z], above),
        (mom_ref.at[0:2, :, 0:2], u.at[1:3, own_x, high_z], below),
        (mag_ref.at[:, :, 2:4], u.at[4:7, own_x, low_z], above),
        (mag_ref.at[:, :, 0:2], u.at[4:7, own_x, high_z], below),
        (mom_ref.at[1:3, 14:16], u.at[2:4, low_x, own_z], up),
        (mom_ref.at[1:3, 0:2], u.at[2:4, high_x, own_z], down),
        (mag_ref.at[:, 14:16], u.at[4:7, low_x, own_z], up),
        (mag_ref.at[:, 0:2], u.at[4:7, high_x, own_z], down),
        (pot_ref.at[14:16], pot.at[6:8], up),
        (pot_ref.at[0:2], pot.at[24:26], down),
    ]
    halos = [send(s, t, halo_s, halo_r, index, w) for index, (s, t, w) in enumerate(pairs)]
    first = 8
    for copy in halos[:first]:
        copy.start()

    for copy in evz:
        copy.wait_recv()
    evx = []
    for index, k in enumerate(xsteps):
        copy = send(
            ev.at[pl.ds(centre, RZ)], ev.at[pl.ds(centre - k * RZ, RZ)], evx_s, evx_r, index,
            {"xy": xy(k)},
        )
        copy.start()
        evx.append(copy)
    for copy in halos[first:]:
        copy.start()
    for copy in evx:
        copy.wait_recv()

    events = ev[...].reshape(SLOTS, 128)
    x0 = (me_xy * XR).astype(F32)
    z0 = (me_gz * ZP).astype(F32)
    nz = float(ngz * ZP)

    def wrapped(value, period):
        value = jnp.where(value >= period / 2, value - period, value)
        return jnp.where(value < -period / 2, value + period, value)

    turned = jnp.transpose(jnp.concatenate([events, events], axis=0))
    ex = wrapped(turned[0:1] - x0, float(NX))
    ez = wrapped(turned[2:3] - z0, nz)
    cell = lax.broadcasted_iota(jnp.int32, (TILE, 128), 0)
    dx = ((cell >> 3) - 2).astype(F32) - ex
    dz = ((cell & 7) - 2).astype(F32) - ez
    room = 256.0 - dx * dx - dz * dz
    second = (lax.broadcasted_iota(jnp.int32, (1, 128), 1) >> 6).astype(F32)
    for t in range(REACH // 2):
        dy = second + float(2 * t - REACH // 2)
        amat[:, 128 * t : 128 * t + 128] = jnp.maximum(room - dy * dy, 0.0).astype(BF16)

    ey = events[:, 1:2]
    en = events[:, 3:4]
    enx = en * wrapped(events[:, 0:1] - x0, float(NX))
    enz = en * wrapped(events[:, 2:3] - z0, nz)
    column = lax.broadcasted_iota(jnp.int32, (SLOTS, NY), 1).astype(F32)

    @pl.loop(0, REACH)
    def _(step):
        dy = (step - REACH // 2).astype(F32)
        hit = ey + dy
        hit = jnp.where(hit < 0.0, hit + float(NY), hit)
        hit = jnp.where(hit >= float(NY), hit - float(NY), hit)
        match = column == hit
        rows = pl.ds(pl.multiple_of(step * SLOTS, SLOTS), SLOTS)
        for which, factor in enumerate((en, enx, en * dy, enz)):
            bmat[rows, which * NY : (which + 1) * NY] = jnp.where(match, factor, 0.0).astype(BF16)

    def total(which):
        return jnp.dot(
            amat[...], bmat[:, which * NY : (which + 1) * NY], preferred_element_type=F32
        )

    here = lax.broadcasted_iota(jnp.int32, (TILE, NY), 0)
    mass = total(0)
    block = (XR + 4, 8, NY)
    src[0] = (mass * (1.0 / 256.0)).reshape(block)
    src[1] = ((((here >> 3) - 2).astype(F32) * mass - total(1)) * (1.0 / 2048.0)).reshape(block)
    src[2] = (total(2) * (1.0 / 2048.0)).reshape(block)
    src[3] = ((((here & 7) - 2).astype(F32) * mass - total(3)) * (1.0 / 2048.0)).reshape(block)

    for copy in local:
        copy.wait()
    for copy in halos[:first]:
        copy.wait_recv()

    def with_source(field, i):
        return u[field, i] + src[field, i]

    def inner(field, i):
        return u[field, i, 2:6] + src[field, i, 2:6]

    @pl.loop(2, XR + 2)
    def _(i):
        rho = with_source(0, i)
        new = (1.0 - 6.0 * DIFF) * rho
        new += DIFF * (with_source(0, i - 1) + with_source(0, i + 1))
        new += ring(with_source(3, i), rho, 0)
        own = new[2:6] + ring(inner(2, i), rho[2:6], 1)
        own += A * (inner(1, i - 2) - inner(1, i + 2))
        own += (8.0 * A) * (inner(1, i + 1) - inner(1, i - 1))
        nd[i - 2] = own

    outs = [pltpu.make_async_copy(nd, orho_ref, out_sem.at[0])]
    outs[0].start()

    high, low = split(nd[...].reshape(XR * ZP, NY))
    both = jnp.dot(jnp.concatenate([high, low], axis=0), hi[...], preferred_element_type=F32)
    rows = XR * ZP
    full = both[:rows] + both[rows:] + jnp.dot(high, lo[...], preferred_element_type=F32)
    for t in range(2 * NY // 128):
        rmat[t] = full[:, 128 * t : 128 * t + 128]

    group = lax.broadcasted_iota(jnp.int32, (XR, 128), 1) >> 4

    @pl.loop(0, NY // 128)
    def _(t):
        parts = []
        for z in range(ZP):
            for half in range(2):
                parts.append(rmat[half * (NY // 128) + t, pl.ds(z, XR, stride=ZP), :])
        for d in range(8):
            value = parts[d]
            for g in range(8):
                if g != d:
                    value = jnp.where(group == g, pltpu.roll(parts[g], (16 * (g - d)) % 128, 1), value)
            outbox[t * 8 + d] = value

    def letter(k):
        peer = xy(k)
        return pltpu.make_async_remote_copy(
            src_ref=outbox.at[peer], dst_ref=inbox.at[me_xy], send_sem=a2a_s.at[k],
            recv_sem=a2a_r.at[k], device_id={"xy": peer}, device_id_type=MESH,
        )

    @pl.loop(1, nxy)
    def _(k):
        letter(k).start()

    inbox[me_xy] = outbox[me_xy]

    for copy in halos[first:]:
        copy.wait_recv()

    @pl.loop(0, XR + 4)
    def _(i):
        rho = with_source(0, i)
        m = [with_source(1 + c, i) for c in range(3)]
        b = [u[4 + c, i] for c in range(3)]
        u[0, i] = rho
        for c in range(3):
            u[1 + c, i] = m[c]
        inverse = 1.0 / rho
        v = [m[c] * inverse for c in range(3)]
        pressure = rho + 0.5 * (b[0] * b[0] + b[1] * b[1] + b[2] * b[2])
        fx[0, i] = m[0] * v[0] - b[0] * b[0] + pressure
        fx[1, i] = m[1] * v[0] - b[1] * b[0]
        fx[2, i] = m[2] * v[0] - b[2] * b[0]
        fx[3, i] = v[0] * b[1] - b[0] * v[1]
        fx[4, i] = v[0] * b[2] - b[0] * v[2]

    @pl.loop(2, XR + 2)
    def _(i):
        rho = u[0, i]
        m = [u[1 + c, i] for c in range(3)]
        b = [u[4 + c, i] for c in range(3)]
        inverse = 1.0 / rho
        v = [m[c] * inverse for c in range(3)]
        pressure = rho + 0.5 * (b[0] * b[0] + b[1] * b[1] + b[2] * b[2])

        def flux(c, k):
            value = m[c] * v[k] - b[c] * b[k]
            return value + pressure if c == k else value

        def along_x(field, which):
            value = DIFF * (u[field, i - 1] + u[field, i + 1])
            if which is not None:
                value += A * (fx[which, i - 2] - fx[which, i + 2])
                value += (8.0 * A) * (fx[which, i + 1] - fx[which, i - 1])
            return value

        def spread(field, axis):
            size = field.shape[axis]
            return DIFF * (pltpu.roll(field, 1, axis) + pltpu.roll(field, size - 1, axis))

        def slope(offset):
            return pot[pl.ds(i + 6 + offset, 1), :]

        keep = 1.0 - 6.0 * DIFF
        for c in range(3):
            new = keep * m[c] + along_x(1 + c, c)
            new += ring(flux(c, 1), m[c], 1)
            new += ring(flux(c, 2), m[c], 0)
            if c == 0:
                pull = A * (slope(-2) - slope(2)) + (8.0 * A) * (slope(1) - slope(-1))
                new += rho * pull
            if c == 1:
                own = jnp.broadcast_to(slope(0), (8, NY))
                pull = A * (pltpu.roll(own, 2, 1) - pltpu.roll(own, NY - 2, 1))
                pull += (8.0 * A) * (pltpu.roll(own, NY - 1, 1) - pltpu.roll(own, 1, 1))
                new += rho * pull
            nmom[c, i - 2] = new[2:6]
        for c in range(3):
            new = keep * b[c] + along_x(4 + c, None if c == 0 else 2 + c)
            if c == 1:
                new += spread(b[c], 1)
            else:
                new += ring(v[1] * b[c] - b[1] * v[c], b[c], 1)
            if c == 2:
                new += spread(b[c], 0)
            else:
                new += ring(v[2] * b[c] - b[2] * v[c], b[c], 0)
            nmag[c, i - 2] = new[2:6]

    outs.append(pltpu.make_async_copy(nmom, omom_ref, out_sem.at[1]))
    outs.append(pltpu.make_async_copy(nmag, omag_ref, out_sem.at[2]))
    outs[1].start()
    outs[2].start()

    @pl.loop(1, nxy)
    def _(k):
        pltpu.make_async_remote_copy(
            src_ref=outbox.at[me_xy], dst_ref=inbox.at[xy(-k)], send_sem=a2a_s.at[k],
            recv_sem=a2a_r.at[k], device_id={"xy": xy(k)}, device_id_type=MESH,
        ).wait_recv()

    high, low = split(inbox[...].reshape(NX, 128))

    def across(lhs, rhs):
        return lax.dot_general(
            lhs, rhs, (((0,), (0,)), ((), ())), preferred_element_type=F32
        )

    both = across(jnp.concatenate([high, low], axis=1), hi[...])
    full = both[:128] + both[128:] + across(high, lo[...])
    scale = 1.0 / 512.0
    wave_y = lax.broadcasted_iota(jnp.int32, (16, NX), 0) + me_xy * 16
    wave_x = lax.broadcasted_iota(jnp.int32, (16, NX), 1)
    origin = (wave_y == 0) & (wave_x == 0)
    for z in range(ZP):
        re = full[32 * z : 32 * z + 16]
        im = full[32 * z + 16 : 32 * z + 32]
        modes[0, z] = jnp.where(origin, 0.0, (re[:, :NX] - im[:, NX:]) * scale)
        modes[1, z] = jnp.where(origin, 0.0, (re[:, NX:] + im[:, :NX]) * -scale)
    outs.append(pltpu.make_async_copy(modes, omode_ref, out_sem.at[3]))
    outs[3].start()

    for copy in evz + evx + halos:
        copy.wait_send()

    @pl.loop(1, nxy)
    def _(k):
        letter(k).wait_send()

    for copy in outs:
        copy.wait()


def on_device(nxy, ngz, high, low, density, momentum, magnetic, arm_potential, sn_cells, sn_counts):
    hbm = pl.BlockSpec(memory_space=pl.ANY)
    smem = pl.BlockSpec(memory_space=pltpu.SMEM)
    halo = 18

    def body(*refs):
        kernel(nxy, ngz, *refs)

    dma = pltpu.SemaphoreType.DMA
    return pl.pallas_call(
        body,
        out_shape=(
            jax.ShapeDtypeStruct((XR, ZP, NY), F32),
            jax.ShapeDtypeStruct((3, XR, ZP, NY), F32),
            jax.ShapeDtypeStruct((3, XR, ZP, NY), F32),
            jax.ShapeDtypeStruct((2, ZP, 16, NX), F32),
        ),
        in_specs=[hbm, hbm, hbm, hbm, smem, smem, hbm, hbm],
        out_specs=(hbm, hbm, hbm, hbm),
        scratch_shapes=[
            pltpu.VMEM((7, XR + 4, 8, NY), F32),
            pltpu.VMEM((4, XR + 4, 8, NY), F32),
            pltpu.VMEM((5, XR + 4, 8, NY), F32),
            pltpu.VMEM((32, NY), F32),
            pltpu.VMEM((SLOTS, 1, 128), F32),
            pltpu.VMEM((TILE, REACH * SLOTS), BF16),
            pltpu.VMEM((REACH * SLOTS, 4 * NY), BF16),
            pltpu.VMEM((NY, 2 * NY), BF16),
            pltpu.VMEM((NY, 2 * NY), BF16),
            pltpu.VMEM((XR, ZP, NY), F32),
            pltpu.VMEM((3, XR, ZP, NY), F32),
            pltpu.VMEM((3, XR, ZP, NY), F32),
            pltpu.VMEM((2 * NY // 128, XR * ZP, 128), F32),
            pltpu.VMEM((nxy, XR, 128), F32),
            pltpu.VMEM((nxy, XR, 128), F32),
            pltpu.VMEM((2, ZP, 16, NX), F32),
            dma((6,)),
            dma((RZ - 1,)), dma((RZ - 1,)),
            dma((RX - 1,)), dma((RX - 1,)),
            dma((halo,)), dma((halo,)),
            dma((nxy,)), dma((nxy,)),
            dma((4,)),
        ],
        compiler_params=pltpu.CompilerParams(
            collective_id=0, has_side_effects=True
        ),
    )(density, momentum, magnetic, arm_potential, sn_cells, sn_counts, high, low)


def solution(mesh):
    nxy, ngz = mesh.shape["xy"], mesh.shape["gz"]
    high, low = tables()

    def step(*arrays):
        return on_device(nxy, ngz, jnp.asarray(high), jnp.asarray(low), *arrays)

    in_specs = (
        P("xy", "gz", None),
        P(None, "xy", "gz", None),
        P(None, "xy", "gz", None),
        P("xy", None),
        P(("gz", "xy"), None),
        P(("gz", "xy")),
    )
    out_specs = (
        P("xy", "gz", None),
        P(None, "xy", "gz", None),
        P(None, "xy", "gz", None),
        P(None, "gz", "xy", None),
    )
    return jax.shard_map(step, mesh=mesh, in_specs=in_specs, out_specs=out_specs, check_vma=False)
```

```python
import jax
import jax.numpy as jnp
import ml_dtypes
import numpy as np
from jax import lax
from jax.experimental import pallas as pl
from jax.experimental.pallas import tpu as pltpu
from jax.sharding import PartitionSpec as P

MESH = pl.DeviceIdType.MESH
F32 = jnp.float32
BF16 = jnp.bfloat16

NX, NY = 512, 512
XR, ZP = 16, 4
RX, RZ = 5, 11
SLOTS = 64
REACH = 16
A = -0.1 / 12.0
DIFF = 0.05
TILE = (XR + 4) * 8


def tables():
    wave = np.arange(NY)
    angle = (wave[:, None] * wave[None, :] % NY) * (2.0 * np.pi / NY)
    full = np.concatenate([np.cos(angle), np.sin(angle)], axis=1)
    high = full.astype(ml_dtypes.bfloat16)
    low = (full - high.astype(np.float64)).astype(ml_dtypes.bfloat16)
    return high, low


def split(value):
    high = value.astype(BF16)
    return high, (value - high.astype(F32)).astype(BF16)


def ring(flux, field, axis):
    size = flux.shape[axis]
    near = DIFF * field
    steep = (8.0 * A) * flux
    far = A * flux
    return (
        pltpu.roll(near - steep, 1, axis)
        + pltpu.roll(near + steep, size - 1, axis)
        + pltpu.roll(far, 2, axis)
        - pltpu.roll(far, size - 2, axis)
    )


def kernel(
    nxy, ngz,
    rho_ref, mom_ref, mag_ref, pot_ref, cells_ref, counts_ref, hi_ref, lo_ref,
    nd, nmom, nmag, modes,
    u, src, fx, pot, ev, amat, bmat, hi, lo, rmat, outbox, inbox,
    local_sem, ev_s, ev_r, halo_s, halo_r, a2a_s, a2a_r,
):
    me_xy = lax.axis_index("xy")
    me_gz = lax.axis_index("gz")

    def xy(k):
        return lax.rem(me_xy + (k + nxy), nxy)

    def gz(k):
        return lax.rem(me_gz + (k + ngz), ngz)

    barrier = pltpu.get_barrier_semaphore()
    middle = (RX * RZ) // 2

    def owner(slot):
        return {"xy": xy(slot // RZ - RX // 2), "gz": gz(lax.rem(slot, RZ) - RZ // 2)}

    def each_other_slot(body):
        pl.loop(0, middle)(body)
        pl.loop(middle + 1, RX * RZ)(body)

    @each_other_slot
    def _(slot):
        pl.semaphore_signal(barrier, inc=1, device_id=owner(slot), device_id_type=MESH)

    @pl.loop(RX // 2 + 1, nxy - RX // 2)
    def _(k):
        pl.semaphore_signal(barrier, inc=1, device_id={"xy": xy(k)}, device_id_type=MESH)

    local = [
        pltpu.make_async_copy(rho_ref, u.at[0, 2:18, 2:6], local_sem.at[0]),
        pltpu.make_async_copy(mom_ref, u.at[1:4, 2:18, 2:6], local_sem.at[1]),
        pltpu.make_async_copy(mag_ref, u.at[4:7, 2:18, 2:6], local_sem.at[2]),
        pltpu.make_async_copy(pot_ref, pot.at[8:24], local_sem.at[3]),
        pltpu.make_async_copy(hi_ref, hi, local_sem.at[4]),
        pltpu.make_async_copy(lo_ref, lo, local_sem.at[5]),
    ]
    for copy in local:
        copy.start()

    lane = lax.broadcasted_iota(jnp.int32, (1, 128), 1)
    row = jnp.where(lane == 0, cells_ref[0, 0], 0)
    row = jnp.where(lane == 1, cells_ref[0, 1], row)
    row = jnp.where(lane == 2, cells_ref[0, 2], row)
    row = jnp.where(lane == 3, counts_ref[0], row)
    ev[middle] = row.astype(F32)
    for slot in range(RX * RZ, SLOTS):
        ev[slot] = jnp.zeros((1, 128), F32)

    pl.semaphore_wait(barrier, RX * RZ - 1 + nxy - RX)

    def send(source, target, sems, recvs, index, where):
        return pltpu.make_async_remote_copy(
            src_ref=source, dst_ref=target, send_sem=sems.at[index], recv_sem=recvs.at[index],
            device_id=where, device_id_type=MESH,
        )

    def event(slot):
        return send(ev.at[middle], ev.at[slot], ev_s, ev_r, slot, owner(RX * RZ - 1 - slot))

    @each_other_slot
    def _(slot):
        event(slot).start()

    up, down = {"xy": xy(1)}, {"xy": xy(-1)}
    above, below = {"gz": gz(1)}, {"gz": gz(-1)}
    low_x, high_x = slice(0, 2), slice(18, 20)
    low_z, high_z = slice(0, 2), slice(6, 8)
    own_x, own_z = slice(2, 18), slice(2, 6)
    pairs = [
        (rho_ref.at[:, 2:4], u.at[0, own_x, low_z], above),
        (rho_ref.at[:, 0:2], u.at[0, own_x, high_z], below),
        (mom_ref.at[2, :, 2:4], u.at[3, own_x, low_z], above),
        (mom_ref.at[2, :, 0:2], u.at[3, own_x, high_z], below),
        (rho_ref.at[14:16], u.at[0, low_x, own_z], up),
        (rho_ref.at[0:2], u.at[0, high_x, own_z], down),
        (mom_ref.at[0, 14:16], u.at[1, low_x, own_z], up),
        (mom_ref.at[0, 0:2], u.at[1, high_x, own_z], down),
        (mom_ref.at[0:2, :, 2:4], u.at[1:3, own_x, low_z], above),
        (mom_ref.at[0:2, :, 0:2], u.at[1:3, own_x, high_z], below),
        (mag_ref.at[:, :, 2:4], u.at[4:7, own_x, low_z], above),
        (mag_ref.at[:, :, 0:2], u.at[4:7, own_x, high_z], below),
        (mom_ref.at[1:3, 14:16], u.at[2:4, low_x, own_z], up),
        (mom_ref.at[1:3, 0:2], u.at[2:4, high_x, own_z], down),
        (mag_ref.at[:, 14:16], u.at[4:7, low_x, own_z], up),
        (mag_ref.at[:, 0:2], u.at[4:7, high_x, own_z], down),
        (pot_ref.at[14:16], pot.at[6:8], up),
        (pot_ref.at[0:2], pot.at[24:26], down),
    ]
    halos = [send(s, t, halo_s, halo_r, index, w) for index, (s, t, w) in enumerate(pairs)]
    first = 8
    for copy in halos[:first]:
        copy.start()

    for copy in halos[first:]:
        copy.start()

    @each_other_slot
    def _(slot):
        event(slot).wait_recv()

    events = ev[...].reshape(SLOTS, 128)
    x0 = (me_xy * XR).astype(F32)
    z0 = (me_gz * ZP).astype(F32)
    nz = float(ngz * ZP)

    def wrapped(value, period):
        value = jnp.where(value >= period / 2, value - period, value)
        return jnp.where(value < -period / 2, value + period, value)

    turned = jnp.transpose(jnp.concatenate([events, events], axis=0))
    ex = wrapped(turned[0:1] - x0, float(NX))
    ez = wrapped(turned[2:3] - z0, nz)
    cell = lax.broadcasted_iota(jnp.int32, (TILE, 128), 0)
    dx = ((cell >> 3) - 2).astype(F32) - ex
    dz = ((cell & 7) - 2).astype(F32) - ez
    room = 256.0 - dx * dx - dz * dz
    second = (lax.broadcasted_iota(jnp.int32, (1, 128), 1) >> 6).astype(F32)
    for t in range(REACH // 2):
        dy = second + float(2 * t)
        amat[:, 128 * t : 128 * t + 128] = jnp.maximum(room - dy * dy, 0.0).astype(BF16)

    en = events[:, 3:4]
    column = lax.broadcasted_iota(jnp.int32, (SLOTS, NY), 1).astype(F32)
    away = wrapped(column - events[:, 1:2], float(NY))
    distance = jnp.abs(away).astype(BF16)
    def wide(value):
        return jnp.where(column >= 0.0, value, 0.0)

    number = wide(en)
    factors = [
        number.astype(BF16),
        (number * wide(wrapped(events[:, 0:1] - x0, float(NX)))).astype(BF16),
        (number * away).astype(BF16),
        (number * wide(wrapped(events[:, 2:3] - z0, nz))).astype(BF16),
    ]
    nothing = jnp.zeros((SLOTS, NY), BF16)
    for step in range(REACH):
        match = distance == jnp.full((SLOTS, NY), step, BF16)
        for which, factor in enumerate(factors):
            bmat[step * SLOTS : (step + 1) * SLOTS, which * NY : (which + 1) * NY] = jnp.where(
                match, factor, nothing
            )

    def total(which):
        return jnp.dot(
            amat[...], bmat[:, which * NY : (which + 1) * NY], preferred_element_type=F32
        )

    here = lax.broadcasted_iota(jnp.int32, (TILE, NY), 0)
    mass = total(0)
    block = (XR + 4, 8, NY)
    src[0] = (mass * (1.0 / 256.0)).reshape(block)
    src[1] = ((((here >> 3) - 2).astype(F32) * mass - total(1)) * (1.0 / 2048.0)).reshape(block)
    src[2] = (total(2) * (1.0 / 2048.0)).reshape(block)
    src[3] = ((((here & 7) - 2).astype(F32) * mass - total(3)) * (1.0 / 2048.0)).reshape(block)

    for copy in local:
        copy.wait()
    for copy in halos[:first]:
        copy.wait_recv()

    def with_source(field, i):
        return u[field, i] + src[field, i]

    def inner(field, i):
        return u[field, i, 2:6] + src[field, i, 2:6]

    @pl.loop(2, XR + 2)
    def _(i):
        rho = with_source(0, i)
        new = (1.0 - 6.0 * DIFF) * rho
        new += DIFF * (with_source(0, i - 1) + with_source(0, i + 1))
        new += ring(with_source(3, i), rho, 0)
        own = new[2:6] + ring(inner(2, i), rho[2:6], 1)
        own += A * (inner(1, i - 2) - inner(1, i + 2))
        own += (8.0 * A) * (inner(1, i + 1) - inner(1, i - 1))
        nd[i - 2] = own

    high, low = split(nd[...].reshape(XR * ZP, NY))
    both = jnp.dot(jnp.concatenate([high, low], axis=0), hi[...], preferred_element_type=F32)
    rows = XR * ZP
    full = both[:rows] + both[rows:] + jnp.dot(high, lo[...], preferred_element_type=F32)
    for t in range(2 * NY // 128):
        rmat[t] = full[:, 128 * t : 128 * t + 128]

    group = lax.broadcasted_iota(jnp.int32, (XR, 128), 1) >> 4

    @pl.loop(0, NY // 128)
    def _(t):
        parts = []
        for z in range(ZP):
            for half in range(2):
                parts.append(rmat[half * (NY // 128) + t, pl.ds(z, XR, stride=ZP), :])
        for d in range(8):
            value = parts[d]
            for g in range(8):
                if g != d:
                    value = jnp.where(group == g, pltpu.roll(parts[g], (16 * (g - d)) % 128, 1), value)
            outbox[t * 8 + d] = value

    def letter(k):
        peer = xy(k)
        return pltpu.make_async_remote_copy(
            src_ref=outbox.at[peer], dst_ref=inbox.at[me_xy], send_sem=a2a_s.at[k],
            recv_sem=a2a_r.at[k], device_id={"xy": peer}, device_id_type=MESH,
        )

    @pl.loop(1, nxy)
    def _(k):
        letter(k).start()

    inbox[me_xy] = outbox[me_xy]

    for copy in halos[first:]:
        copy.wait_recv()

    @pl.loop(0, XR + 4)
    def _(i):
        rho = with_source(0, i)
        m = [with_source(1 + c, i) for c in range(3)]
        b = [u[4 + c, i] for c in range(3)]
        u[0, i] = rho
        for c in range(3):
            u[1 + c, i] = m[c]
        inverse = 1.0 / rho
        v = [m[c] * inverse for c in range(3)]
        pressure = rho + 0.5 * (b[0] * b[0] + b[1] * b[1] + b[2] * b[2])
        fx[0, i] = m[0] * v[0] - b[0] * b[0] + pressure
        fx[1, i] = m[1] * v[0] - b[1] * b[0]
        fx[2, i] = m[2] * v[0] - b[2] * b[0]
        fx[3, i] = v[0] * b[1] - b[0] * v[1]
        fx[4, i] = v[0] * b[2] - b[0] * v[2]

    @pl.loop(2, XR + 2)
    def _(i):
        rho = u[0, i]
        m = [u[1 + c, i] for c in range(3)]
        b = [u[4 + c, i] for c in range(3)]
        inverse = 1.0 / rho
        v = [m[c] * inverse for c in range(3)]
        pressure = rho + 0.5 * (b[0] * b[0] + b[1] * b[1] + b[2] * b[2])

        def flux(c, k):
            value = m[c] * v[k] - b[c] * b[k]
            return value + pressure if c == k else value

        def along_x(field, which):
            value = DIFF * (u[field, i - 1] + u[field, i + 1])
            if which is not None:
                value += A * (fx[which, i - 2] - fx[which, i + 2])
                value += (8.0 * A) * (fx[which, i + 1] - fx[which, i - 1])
            return value

        def spread(field, axis):
            size = field.shape[axis]
            return DIFF * (pltpu.roll(field, 1, axis) + pltpu.roll(field, size - 1, axis))

        def slope(offset):
            return pot[pl.ds(i + 6 + offset, 1), :]

        keep = 1.0 - 6.0 * DIFF
        for c in range(3):
            new = keep * m[c] + along_x(1 + c, c)
            new += ring(flux(c, 1), m[c], 1)
            new += ring(flux(c, 2), m[c], 0)
            if c == 0:
                pull = A * (slope(-2) - slope(2)) + (8.0 * A) * (slope(1) - slope(-1))
                new += rho * pull
            if c == 1:
                own = jnp.broadcast_to(slope(0), (8, NY))
                pull = A * (pltpu.roll(own, 2, 1) - pltpu.roll(own, NY - 2, 1))
                pull += (8.0 * A) * (pltpu.roll(own, NY - 1, 1) - pltpu.roll(own, 1, 1))
                new += rho * pull
            nmom[c, i - 2] = new[2:6]
        for c in range(3):
            new = keep * b[c] + along_x(4 + c, None if c == 0 else 2 + c)
            if c == 1:
                new += spread(b[c], 1)
            else:
                new += ring(v[1] * b[c] - b[1] * v[c], b[c], 1)
            if c == 2:
                new += spread(b[c], 0)
            else:
                new += ring(v[2] * b[c] - b[2] * v[c], b[c], 0)
            nmag[c, i - 2] = new[2:6]

    @pl.loop(1, nxy)
    def _(k):
        pltpu.make_async_remote_copy(
            src_ref=outbox.at[me_xy], dst_ref=inbox.at[xy(-k)], send_sem=a2a_s.at[k],
            recv_sem=a2a_r.at[k], device_id={"xy": xy(k)}, device_id_type=MESH,
        ).wait_recv()

    high, low = split(inbox[...].reshape(NX, 128))

    def across(lhs, rhs):
        return lax.dot_general(
            lhs, rhs, (((0,), (0,)), ((), ())), preferred_element_type=F32
        )

    both = across(jnp.concatenate([high, low], axis=1), hi[...])
    full = both[:128] + both[128:] + across(high, lo[...])
    scale = 1.0 / 512.0
    wave_y = lax.broadcasted_iota(jnp.int32, (16, NX), 0) + me_xy * 16
    wave_x = lax.broadcasted_iota(jnp.int32, (16, NX), 1)
    origin = (wave_y == 0) & (wave_x == 0)
    for z in range(ZP):
        re = full[32 * z : 32 * z + 16]
        im = full[32 * z + 16 : 32 * z + 32]
        modes[0, z] = jnp.where(origin, 0.0, (re[:, :NX] - im[:, NX:]) * scale)
        modes[1, z] = jnp.where(origin, 0.0, (re[:, NX:] + im[:, :NX]) * -scale)

    for copy in halos:
        copy.wait_send()

    @each_other_slot
    def _(slot):
        event(slot).wait_send()

    @pl.loop(1, nxy)
    def _(k):
        letter(k).wait_send()


def deliver(*refs):
    count = (len(refs) - 1) // 2
    sems = refs[-1]
    copies = [
        pltpu.make_async_copy(refs[i], refs[count + i], sems.at[i]) for i in range(count)
    ]
    for copy in copies:
        copy.start()
    for copy in copies:
        copy.wait()


def on_device(nxy, ngz, high, low, density, momentum, magnetic, arm_potential, sn_cells, sn_counts):
    hbm = pl.BlockSpec(memory_space=pl.ANY)
    smem = pl.BlockSpec(memory_space=pltpu.SMEM)
    halo = 18

    def body(*refs):
        kernel(nxy, ngz, *refs)

    dma = pltpu.SemaphoreType.DMA
    shapes = ((XR, ZP, NY), (3, XR, ZP, NY), (3, XR, ZP, NY), (2, ZP, 16, NX))
    results = pl.pallas_call(
        body,
        out_shape=tuple(pltpu.VMEM(shape, F32) for shape in shapes),
        in_specs=[hbm, hbm, hbm, hbm, smem, smem, hbm, hbm],
        out_specs=tuple(pl.BlockSpec(memory_space=pltpu.VMEM) for _ in shapes),
        scratch_shapes=[
            pltpu.VMEM((7, XR + 4, 8, NY), F32),
            pltpu.VMEM((4, XR + 4, 8, NY), F32),
            pltpu.VMEM((5, XR + 4, 8, NY), F32),
            pltpu.VMEM((32, NY), F32),
            pltpu.VMEM((SLOTS, 1, 128), F32),
            pltpu.VMEM((TILE, REACH * SLOTS), BF16),
            pltpu.VMEM((REACH * SLOTS, 4 * NY), BF16),
            pltpu.VMEM((NY, 2 * NY), BF16),
            pltpu.VMEM((NY, 2 * NY), BF16),
            pltpu.VMEM((2 * NY // 128, XR * ZP, 128), F32),
            pltpu.VMEM((nxy, XR, 128), F32),
            pltpu.VMEM((nxy, XR, 128), F32),
            dma((6,)),
            dma((RX * RZ,)), dma((RX * RZ,)),
            dma((halo,)), dma((halo,)),
            dma((nxy,)), dma((nxy,)),
        ],
        compiler_params=pltpu.CompilerParams(collective_id=0, has_side_effects=True),
    )(density, momentum, magnetic, arm_potential, sn_cells, sn_counts, high, low)
    return pl.pallas_call(
        deliver,
        out_shape=tuple(jax.ShapeDtypeStruct(shape, F32) for shape in shapes),
        in_specs=[hbm] * 4,
        out_specs=(hbm,) * 4,
        scratch_shapes=[dma((4,))],
        compiler_params=pltpu.CompilerParams(vmem_limit_bytes=16 * 1024 * 1024),
    )(*results)


def solution(mesh):
    nxy, ngz = mesh.shape["xy"], mesh.shape["gz"]
    high, low = tables()

    def step(*arrays):
        return on_device(nxy, ngz, jnp.asarray(high), jnp.asarray(low), *arrays)

    in_specs = (
        P("xy", "gz", None),
        P(None, "xy", "gz", None),
        P(None, "xy", "gz", None),
        P("xy", None),
        P(("gz", "xy"), None),
        P(("gz", "xy")),
    )
    out_specs = (
        P("xy", "gz", None),
        P(None, "xy", "gz", None),
        P(None, "xy", "gz", None),
        P(None, "gz", "xy", None),
    )
    return jax.shard_map(step, mesh=mesh, in_specs=in_specs, out_specs=out_specs, check_vma=False)
```

```python
import jax
import jax.numpy as jnp
import ml_dtypes
import numpy as np
from jax import lax
from jax.experimental import pallas as pl
from jax.experimental.pallas import tpu as pltpu
from jax.sharding import PartitionSpec as P

MESH = pl.DeviceIdType.MESH
F32 = jnp.float32
BF16 = jnp.bfloat16

NX, NY = 512, 512
XR, ZP = 16, 4
RX, RZ = 5, 11
SLOTS = 64
REACH = 16
A = -0.1 / 12.0
DIFF = 0.05
TILE = (XR + 4) * 8


def tables():
    wave = np.arange(NY)
    angle = (wave[:, None] * wave[None, :] % NY) * (2.0 * np.pi / NY)
    full = np.concatenate([np.cos(angle), np.sin(angle)], axis=1)
    high = full.astype(ml_dtypes.bfloat16)
    low = (full - high.astype(np.float64)).astype(ml_dtypes.bfloat16)
    return high, low


def split(value):
    high = value.astype(BF16)
    return high, (value - high.astype(F32)).astype(BF16)


def ring(flux, field, axis):
    size = flux.shape[axis]
    near = DIFF * field
    steep = (8.0 * A) * flux
    far = A * flux
    return (
        pltpu.roll(near - steep, 1, axis)
        + pltpu.roll(near + steep, size - 1, axis)
        + pltpu.roll(far, 2, axis)
        - pltpu.roll(far, size - 2, axis)
    )


def kernel(
    nxy, ngz,
    rho_ref, mom_ref, mag_ref, pot_ref, cells_ref, counts_ref, hi_ref, lo_ref,
    nd, nmom, nmag, modes,
    u, src, fx, pot, ev, amat, bmat, hi, lo, rmat, outbox, inbox,
    local_sem, ev_s, ev_r, halo_s, halo_r, a2a_s, a2a_r,
):
    me_xy = lax.axis_index("xy")
    me_gz = lax.axis_index("gz")

    def shifted(me, k, size):
        there = me + k
        if k < 0:
            return jnp.where(there < 0, there + size, there)
        return jnp.where(there >= size, there - size, there)

    row_of = {k: shifted(me_xy, k, nxy) for k in range(-(nxy // 2), nxy - nxy // 2)}
    plane_of = {k: shifted(me_gz, k, ngz) for k in range(-(RZ // 2), RZ // 2 + 1)}
    peers = sorted((k for k in row_of if k), key=lambda k: (-abs(k), k))

    barrier = pltpu.get_barrier_semaphore()
    middle = (RX * RZ) // 2
    slots = [slot for slot in range(RX * RZ) if slot != middle]

    def owner(slot):
        return {"xy": row_of[slot // RZ - RX // 2], "gz": plane_of[slot % RZ - RZ // 2]}

    beyond = [k for k in peers if abs(k) > RX // 2]
    for slot in slots:
        pl.semaphore_signal(barrier, inc=1, device_id=owner(slot), device_id_type=MESH)
    for k in beyond:
        pl.semaphore_signal(barrier, inc=1, device_id={"xy": row_of[k]}, device_id_type=MESH)

    local = [
        pltpu.make_async_copy(rho_ref, u.at[0, 2:18, 2:6], local_sem.at[0]),
        pltpu.make_async_copy(mom_ref, u.at[1:4, 2:18, 2:6], local_sem.at[1]),
        pltpu.make_async_copy(mag_ref, u.at[4:7, 2:18, 2:6], local_sem.at[2]),
        pltpu.make_async_copy(pot_ref, pot.at[8:24], local_sem.at[3]),
        pltpu.make_async_copy(hi_ref, hi, local_sem.at[4]),
        pltpu.make_async_copy(lo_ref, lo, local_sem.at[5]),
    ]
    for copy in local:
        copy.start()

    lane = lax.broadcasted_iota(jnp.int32, (1, 128), 1)
    row = jnp.where(lane == 0, cells_ref[0, 0], 0)
    row = jnp.where(lane == 1, cells_ref[0, 1], row)
    row = jnp.where(lane == 2, cells_ref[0, 2], row)
    row = jnp.where(lane == 3, counts_ref[0], row)
    ev[middle] = row.astype(F32)
    for slot in range(RX * RZ, SLOTS):
        ev[slot] = jnp.zeros((1, 128), F32)

    pl.semaphore_wait(barrier, len(slots) + len(beyond))

    def send(source, target, sems, recvs, index, where):
        return pltpu.make_async_remote_copy(
            src_ref=source, dst_ref=target, send_sem=sems.at[index], recv_sem=recvs.at[index],
            device_id=where, device_id_type=MESH,
        )

    def event(slot):
        return send(ev.at[middle], ev.at[slot], ev_s, ev_r, slot, owner(RX * RZ - 1 - slot))

    for slot in slots:
        event(slot).start()

    up, down = {"xy": row_of[1]}, {"xy": row_of[-1]}
    above, below = {"gz": plane_of[1]}, {"gz": plane_of[-1]}
    low_x, high_x = slice(0, 2), slice(18, 20)
    low_z, high_z = slice(0, 2), slice(6, 8)
    own_x, own_z = slice(2, 18), slice(2, 6)
    pairs = [
        (rho_ref.at[:, 2:4], u.at[0, own_x, low_z], above),
        (rho_ref.at[:, 0:2], u.at[0, own_x, high_z], below),
        (mom_ref.at[2, :, 2:4], u.at[3, own_x, low_z], above),
        (mom_ref.at[2, :, 0:2], u.at[3, own_x, high_z], below),
        (rho_ref.at[14:16], u.at[0, low_x, own_z], up),
        (rho_ref.at[0:2], u.at[0, high_x, own_z], down),
        (mom_ref.at[0, 14:16], u.at[1, low_x, own_z], up),
        (mom_ref.at[0, 0:2], u.at[1, high_x, own_z], down),
        (mom_ref.at[0:2, :, 2:4], u.at[1:3, own_x, low_z], above),
        (mom_ref.at[0:2, :, 0:2], u.at[1:3, own_x, high_z], below),
        (mag_ref.at[:, :, 2:4], u.at[4:7, own_x, low_z], above),
        (mag_ref.at[:, :, 0:2], u.at[4:7, own_x, high_z], below),
        (mom_ref.at[1:3, 14:16], u.at[2:4, low_x, own_z], up),
        (mom_ref.at[1:3, 0:2], u.at[2:4, high_x, own_z], down),
        (mag_ref.at[:, 14:16], u.at[4:7, low_x, own_z], up),
        (mag_ref.at[:, 0:2], u.at[4:7, high_x, own_z], down),
        (pot_ref.at[14:16], pot.at[6:8], up),
        (pot_ref.at[0:2], pot.at[24:26], down),
    ]
    halos = [send(s, t, halo_s, halo_r, index, w) for index, (s, t, w) in enumerate(pairs)]
    first = 8
    for copy in halos[:first]:
        copy.start()

    for copy in halos[first:]:
        copy.start()

    for slot in slots:
        event(slot).wait_recv()

    events = ev[...].reshape(SLOTS, 128)
    x0 = (me_xy * XR).astype(F32)
    z0 = (me_gz * ZP).astype(F32)
    nz = float(ngz * ZP)

    def wrapped(value, period):
        value = jnp.where(value >= period / 2, value - period, value)
        return jnp.where(value < -period / 2, value + period, value)

    turned = jnp.transpose(jnp.concatenate([events, events], axis=0))
    ex = wrapped(turned[0:1] - x0, float(NX))
    ez = wrapped(turned[2:3] - z0, nz)
    cell = lax.broadcasted_iota(jnp.int32, (TILE, 128), 0)
    dx = ((cell >> 3) - 2).astype(F32) - ex
    dz = ((cell & 7) - 2).astype(F32) - ez
    room = 256.0 - dx * dx - dz * dz
    second = (lax.broadcasted_iota(jnp.int32, (1, 128), 1) >> 6).astype(F32)
    for t in range(REACH // 2):
        dy = second + float(2 * t)
        amat[:, 128 * t : 128 * t + 128] = jnp.maximum(room - dy * dy, 0.0).astype(BF16)

    en = events[:, 3:4]
    column = lax.broadcasted_iota(jnp.int32, (SLOTS, NY), 1).astype(F32)
    away = wrapped(column - events[:, 1:2], float(NY))
    distance = jnp.abs(away).astype(BF16)
    def wide(value):
        return jnp.where(column >= 0.0, value, 0.0)

    number = wide(en)
    factors = [
        number.astype(BF16),
        (number * wide(wrapped(events[:, 0:1] - x0, float(NX)))).astype(BF16),
        (number * away).astype(BF16),
        (number * wide(wrapped(events[:, 2:3] - z0, nz))).astype(BF16),
    ]
    nothing = jnp.zeros((SLOTS, NY), BF16)
    for step in range(REACH):
        match = distance == jnp.full((SLOTS, NY), step, BF16)
        for which, factor in enumerate(factors):
            bmat[step * SLOTS : (step + 1) * SLOTS, which * NY : (which + 1) * NY] = jnp.where(
                match, factor, nothing
            )

    def total(which):
        return jnp.dot(
            amat[...], bmat[:, which * NY : (which + 1) * NY], preferred_element_type=F32
        )

    here = lax.broadcasted_iota(jnp.int32, (TILE, NY), 0)
    mass = total(0)
    block = (XR + 4, 8, NY)
    src[0] = (mass * (1.0 / 256.0)).reshape(block)
    src[1] = ((((here >> 3) - 2).astype(F32) * mass - total(1)) * (1.0 / 2048.0)).reshape(block)
    src[2] = (total(2) * (1.0 / 2048.0)).reshape(block)
    src[3] = ((((here & 7) - 2).astype(F32) * mass - total(3)) * (1.0 / 2048.0)).reshape(block)

    for copy in local:
        copy.wait()
    for copy in halos[:first]:
        copy.wait_recv()

    def with_source(field, i):
        return u[field, i] + src[field, i]

    def inner(field, i):
        return u[field, i, 2:6] + src[field, i, 2:6]

    @pl.loop(2, XR + 2)
    def _(i):
        rho = with_source(0, i)
        new = (1.0 - 6.0 * DIFF) * rho
        new += DIFF * (with_source(0, i - 1) + with_source(0, i + 1))
        new += ring(with_source(3, i), rho, 0)
        own = new[2:6] + ring(inner(2, i), rho[2:6], 1)
        own += A * (inner(1, i - 2) - inner(1, i + 2))
        own += (8.0 * A) * (inner(1, i + 1) - inner(1, i - 1))
        nd[i - 2] = own

    high, low = split(nd[...].reshape(XR * ZP, NY))
    both = jnp.dot(jnp.concatenate([high, low], axis=0), hi[...], preferred_element_type=F32)
    rows = XR * ZP
    full = both[:rows] + both[rows:] + jnp.dot(high, lo[...], preferred_element_type=F32)
    for t in range(2 * NY // 128):
        rmat[t] = full[:, 128 * t : 128 * t + 128]

    group = lax.broadcasted_iota(jnp.int32, (XR, 128), 1) >> 4

    @pl.loop(0, NY // 128)
    def _(t):
        parts = []
        for z in range(ZP):
            for half in range(2):
                parts.append(rmat[half * (NY // 128) + t, pl.ds(z, XR, stride=ZP), :])
        for d in range(8):
            value = parts[d]
            for g in range(8):
                if g != d:
                    value = jnp.where(group == g, pltpu.roll(parts[g], (16 * (g - d)) % 128, 1), value)
            outbox[t * 8 + d] = value

    def letter(k):
        return pltpu.make_async_remote_copy(
            src_ref=outbox.at[row_of[k]], dst_ref=inbox.at[me_xy], send_sem=a2a_s.at[k % nxy],
            recv_sem=a2a_r.at[k % nxy], device_id={"xy": row_of[k]}, device_id_type=MESH,
        )

    letters = [letter(k) for k in peers]
    for copy in letters:
        copy.start()

    inbox[me_xy] = outbox[me_xy]

    for copy in halos[first:]:
        copy.wait_recv()

    @pl.loop(0, XR + 4)
    def _(i):
        rho = with_source(0, i)
        m = [with_source(1 + c, i) for c in range(3)]
        b = [u[4 + c, i] for c in range(3)]
        u[0, i] = rho
        for c in range(3):
            u[1 + c, i] = m[c]
        inverse = 1.0 / rho
        v = [m[c] * inverse for c in range(3)]
        pressure = rho + 0.5 * (b[0] * b[0] + b[1] * b[1] + b[2] * b[2])
        fx[0, i] = m[0] * v[0] - b[0] * b[0] + pressure
        fx[1, i] = m[1] * v[0] - b[1] * b[0]
        fx[2, i] = m[2] * v[0] - b[2] * b[0]
        fx[3, i] = v[0] * b[1] - b[0] * v[1]
        fx[4, i] = v[0] * b[2] - b[0] * v[2]

    @pl.loop(2, XR + 2)
    def _(i):
        rho = u[0, i]
        m = [u[1 + c, i] for c in range(3)]
        b = [u[4 + c, i] for c in range(3)]
        inverse = 1.0 / rho
        v = [m[c] * inverse for c in range(3)]
        pressure = rho + 0.5 * (b[0] * b[0] + b[1] * b[1] + b[2] * b[2])

        def flux(c, k):
            value = m[c] * v[k] - b[c] * b[k]
            return value + pressure if c == k else value

        def along_x(field, which):
            value = DIFF * (u[field, i - 1] + u[field, i + 1])
            if which is not None:
                value += A * (fx[which, i - 2] - fx[which, i + 2])
                value += (8.0 * A) * (fx[which, i + 1] - fx[which, i - 1])
            return value

        def spread(field, axis):
            size = field.shape[axis]
            return DIFF * (pltpu.roll(field, 1, axis) + pltpu.roll(field, size - 1, axis))

        def slope(offset):
            return pot[pl.ds(i + 6 + offset, 1), :]

        keep = 1.0 - 6.0 * DIFF
        for c in range(3):
            new = keep * m[c] + along_x(1 + c, c)
            new += ring(flux(c, 1), m[c], 1)
            new += ring(flux(c, 2), m[c], 0)
            if c == 0:
                pull = A * (slope(-2) - slope(2)) + (8.0 * A) * (slope(1) - slope(-1))
                new += rho * pull
            if c == 1:
                own = jnp.broadcast_to(slope(0), (8, NY))
                pull = A * (pltpu.roll(own, 2, 1) - pltpu.roll(own, NY - 2, 1))
                pull += (8.0 * A) * (pltpu.roll(own, NY - 1, 1) - pltpu.roll(own, 1, 1))
                new += rho * pull
            nmom[c, i - 2] = new[2:6]
        for c in range(3):
            new = keep * b[c] + along_x(4 + c, None if c == 0 else 2 + c)
            if c == 1:
                new += spread(b[c], 1)
            else:
                new += ring(v[1] * b[c] - b[1] * v[c], b[c], 1)
            if c == 2:
                new += spread(b[c], 0)
            else:
                new += ring(v[2] * b[c] - b[2] * v[c], b[c], 0)
            nmag[c, i - 2] = new[2:6]

    for copy in letters:
        copy.wait_recv()

    high, low = split(inbox[...].reshape(NX, 128))

    def across(lhs, rhs):
        return lax.dot_general(
            lhs, rhs, (((0,), (0,)), ((), ())), preferred_element_type=F32
        )

    both = across(jnp.concatenate([high, low], axis=1), hi[...])
    full = both[:128] + both[128:] + across(high, lo[...])
    scale = 1.0 / 512.0
    wave_y = lax.broadcasted_iota(jnp.int32, (16, NX), 0) + me_xy * 16
    wave_x = lax.broadcasted_iota(jnp.int32, (16, NX), 1)
    origin = (wave_y == 0) & (wave_x == 0)
    for z in range(ZP):
        re = full[32 * z : 32 * z + 16]
        im = full[32 * z + 16 : 32 * z + 32]
        modes[0, z] = jnp.where(origin, 0.0, (re[:, :NX] - im[:, NX:]) * scale)
        modes[1, z] = jnp.where(origin, 0.0, (re[:, NX:] + im[:, :NX]) * -scale)

    for copy in halos:
        copy.wait_send()

    for slot in slots:
        event(slot).wait_send()

    for copy in letters:
        copy.wait_send()


def deliver(*refs):
    count = (len(refs) - 1) // 2
    sems = refs[-1]
    copies = [
        pltpu.make_async_copy(refs[i], refs[count + i], sems.at[i]) for i in range(count)
    ]
    for copy in copies:
        copy.start()
    for copy in copies:
        copy.wait()


def on_device(nxy, ngz, high, low, density, momentum, magnetic, arm_potential, sn_cells, sn_counts):
    hbm = pl.BlockSpec(memory_space=pl.ANY)
    smem = pl.BlockSpec(memory_space=pltpu.SMEM)
    halo = 18

    def body(*refs):
        kernel(nxy, ngz, *refs)

    dma = pltpu.SemaphoreType.DMA
    shapes = ((XR, ZP, NY), (3, XR, ZP, NY), (3, XR, ZP, NY), (2, ZP, 16, NX))
    results = pl.pallas_call(
        body,
        out_shape=tuple(pltpu.VMEM(shape, F32) for shape in shapes),
        in_specs=[hbm, hbm, hbm, hbm, smem, smem, hbm, hbm],
        out_specs=tuple(pl.BlockSpec(memory_space=pltpu.VMEM) for _ in shapes),
        scratch_shapes=[
            pltpu.VMEM((7, XR + 4, 8, NY), F32),
            pltpu.VMEM((4, XR + 4, 8, NY), F32),
            pltpu.VMEM((5, XR + 4, 8, NY), F32),
            pltpu.VMEM((32, NY), F32),
            pltpu.VMEM((SLOTS, 1, 128), F32),
            pltpu.VMEM((TILE, REACH * SLOTS), BF16),
            pltpu.VMEM((REACH * SLOTS, 4 * NY), BF16),
            pltpu.VMEM((NY, 2 * NY), BF16),
            pltpu.VMEM((NY, 2 * NY), BF16),
            pltpu.VMEM((2 * NY // 128, XR * ZP, 128), F32),
            pltpu.VMEM((nxy, XR, 128), F32),
            pltpu.VMEM((nxy, XR, 128), F32),
            dma((6,)),
            dma((RX * RZ,)), dma((RX * RZ,)),
            dma((halo,)), dma((halo,)),
            dma((nxy,)), dma((nxy,)),
        ],
        compiler_params=pltpu.CompilerParams(collective_id=0, has_side_effects=True),
    )(density, momentum, magnetic, arm_potential, sn_cells, sn_counts, high, low)
    return pl.pallas_call(
        deliver,
        out_shape=tuple(jax.ShapeDtypeStruct(shape, F32) for shape in shapes),
        in_specs=[hbm] * 4,
        out_specs=(hbm,) * 4,
        scratch_shapes=[dma((4,))],
        compiler_params=pltpu.CompilerParams(vmem_limit_bytes=16 * 1024 * 1024),
    )(*results)


def solution(mesh):
    nxy, ngz = mesh.shape["xy"], mesh.shape["gz"]
    high, low = tables()

    def step(*arrays):
        return on_device(nxy, ngz, jnp.asarray(high), jnp.asarray(low), *arrays)

    in_specs = (
        P("xy", "gz", None),
        P(None, "xy", "gz", None),
        P(None, "xy", "gz", None),
        P("xy", None),
        P(("gz", "xy"), None),
        P(("gz", "xy")),
    )
    out_specs = (
        P("xy", "gz", None),
        P(None, "xy", "gz", None),
        P(None, "xy", "gz", None),
        P(None, "gz", "xy", None),
    )
    return jax.shard_map(step, mesh=mesh, in_specs=in_specs, out_specs=out_specs, check_vma=False)
```

```python
import jax
import jax.numpy as jnp
import ml_dtypes
import numpy as np
from jax import lax
from jax.experimental import pallas as pl
from jax.experimental.pallas import tpu as pltpu
from jax.sharding import PartitionSpec as P

MESH = pl.DeviceIdType.MESH
F32 = jnp.float32
BF16 = jnp.bfloat16

NX, NY = 512, 512
XR, ZP = 16, 4
RX, RZ = 5, 11
SLOTS = 64
REACH = 16
TORUS_X = 4
A = -0.1 / 12.0
DIFF = 0.05
TILE = (XR + 4) * 8


def tables():
    wave = np.arange(NY)
    angle = (wave[:, None] * wave[None, :] % NY) * (2.0 * np.pi / NY)
    full = np.concatenate([np.cos(angle), np.sin(angle)], axis=1)
    high = full.astype(ml_dtypes.bfloat16)
    low = (full - high.astype(np.float64)).astype(ml_dtypes.bfloat16)
    return high, low


def split(value):
    high = value.astype(BF16)
    return high, (value - high.astype(F32)).astype(BF16)


def ring(flux, field, axis):
    size = flux.shape[axis]
    near = DIFF * field
    steep = (8.0 * A) * flux
    far = A * flux
    return (
        pltpu.roll(near - steep, 1, axis)
        + pltpu.roll(near + steep, size - 1, axis)
        + pltpu.roll(far, 2, axis)
        - pltpu.roll(far, size - 2, axis)
    )


def kernel(
    nxy, ngz,
    rho_ref, mom_ref, mag_ref, pot_ref, cells_ref, counts_ref, hi_ref, lo_ref,
    nd, nmom, nmag, modes,
    u, src, fx, pot, ev, amat, bmat, hi, lo, rmat, outbox, inbox,
    local_sem, ev_s, ev_r, halo_s, halo_r, a2a_s, a2a_r,
):
    me_xy = lax.axis_index("xy")
    me_gz = lax.axis_index("gz")

    def shifted(me, k, size):
        there = me + k
        if k < 0:
            return jnp.where(there < 0, there + size, there)
        return jnp.where(there >= size, there - size, there)

    row_of = {k: shifted(me_xy, k, nxy) for k in range(-(nxy // 2), nxy - nxy // 2)}
    plane_of = {k: shifted(me_gz, k, ngz) for k in range(-(RZ // 2), RZ // 2 + 1)}
    peers = sorted((k for k in row_of if k), key=lambda k: (-abs(k), k))

    ny = nxy // TORUS_X
    me_y = me_xy // TORUS_X
    me_x = me_xy - TORUS_X * me_y
    y_order = [ny // 2] + [sign * k for k in range(ny // 2 - 1, 0, -1) for sign in (-1, 1)] + [0]
    peer_ids = [
        shifted(me_y, dy, ny) * TORUS_X + shifted(me_x, dx, TORUS_X)
        for dx in (2, 1, 3, 0)
        for dy in y_order
        if dx or dy
    ]

    barrier = pltpu.get_barrier_semaphore()
    middle = (RX * RZ) // 2
    slots = [slot for slot in range(RX * RZ) if slot != middle]

    def owner(slot):
        return {"xy": row_of[slot // RZ - RX // 2], "gz": plane_of[slot % RZ - RZ // 2]}

    beyond = [k for k in peers if abs(k) > RX // 2]
    for slot in slots:
        pl.semaphore_signal(barrier, inc=1, device_id=owner(slot), device_id_type=MESH)
    for k in beyond:
        pl.semaphore_signal(barrier, inc=1, device_id={"xy": row_of[k]}, device_id_type=MESH)

    local = [
        pltpu.make_async_copy(rho_ref, u.at[0, 2:18, 2:6], local_sem.at[0]),
        pltpu.make_async_copy(mom_ref, u.at[1:4, 2:18, 2:6], local_sem.at[1]),
        pltpu.make_async_copy(mag_ref, u.at[4:7, 2:18, 2:6], local_sem.at[2]),
        pltpu.make_async_copy(pot_ref, pot.at[8:24], local_sem.at[3]),
        pltpu.make_async_copy(hi_ref, hi, local_sem.at[4]),
        pltpu.make_async_copy(lo_ref, lo, local_sem.at[5]),
    ]
    for copy in local:
        copy.start()

    lane = lax.broadcasted_iota(jnp.int32, (1, 128), 1)
    row = jnp.where(lane == 0, cells_ref[0, 0], 0)
    row = jnp.where(lane == 1, cells_ref[0, 1], row)
    row = jnp.where(lane == 2, cells_ref[0, 2], row)
    row = jnp.where(lane == 3, counts_ref[0], row)
    ev[middle] = row.astype(F32)
    for slot in range(RX * RZ, SLOTS):
        ev[slot] = jnp.zeros((1, 128), F32)

    pl.semaphore_wait(barrier, len(slots) + len(beyond))

    def send(source, target, sems, recvs, index, where):
        return pltpu.make_async_remote_copy(
            src_ref=source, dst_ref=target, send_sem=sems.at[index], recv_sem=recvs.at[index],
            device_id=where, device_id_type=MESH,
        )

    def drain(sem, ref):
        pltpu.make_async_copy(ref, ref, sem).wait()

    def event(slot):
        return send(ev.at[middle], ev.at[slot], ev_s, ev_r, 0, owner(RX * RZ - 1 - slot))

    for slot in slots:
        event(slot).start()

    up, down = {"xy": row_of[1]}, {"xy": row_of[-1]}
    above, below = {"gz": plane_of[1]}, {"gz": plane_of[-1]}
    low_x, high_x = slice(0, 2), slice(18, 20)
    low_z, high_z = slice(0, 2), slice(6, 8)
    own_x, own_z = slice(2, 18), slice(2, 6)
    pairs = [
        (rho_ref.at[:, 2:4], u.at[0, own_x, low_z], above),
        (rho_ref.at[:, 0:2], u.at[0, own_x, high_z], below),
        (mom_ref.at[2, :, 2:4], u.at[3, own_x, low_z], above),
        (mom_ref.at[2, :, 0:2], u.at[3, own_x, high_z], below),
        (rho_ref.at[14:16], u.at[0, low_x, own_z], up),
        (rho_ref.at[0:2], u.at[0, high_x, own_z], down),
        (mom_ref.at[0, 14:16], u.at[1, low_x, own_z], up),
        (mom_ref.at[0, 0:2], u.at[1, high_x, own_z], down),
        (mom_ref.at[0:2, :, 2:4], u.at[1:3, own_x, low_z], above),
        (mom_ref.at[0:2, :, 0:2], u.at[1:3, own_x, high_z], below),
        (mag_ref.at[:, :, 2:4], u.at[4:7, own_x, low_z], above),
        (mag_ref.at[:, :, 0:2], u.at[4:7, own_x, high_z], below),
        (mom_ref.at[1:3, 14:16], u.at[2:4, low_x, own_z], up),
        (mom_ref.at[1:3, 0:2], u.at[2:4, high_x, own_z], down),
        (mag_ref.at[:, 14:16], u.at[4:7, low_x, own_z], up),
        (mag_ref.at[:, 0:2], u.at[4:7, high_x, own_z], down),
        (pot_ref.at[14:16], pot.at[6:8], up),
        (pot_ref.at[0:2], pot.at[24:26], down),
    ]
    halos = [send(s, t, halo_s, halo_r, index, w) for index, (s, t, w) in enumerate(pairs)]
    first = 8
    for copy in halos[:first]:
        copy.start()

    for copy in halos[first:]:
        copy.start()

    drain(ev_r.at[0], ev.at[0 : len(slots)])

    events = ev[...].reshape(SLOTS, 128)
    x0 = (me_xy * XR).astype(F32)
    z0 = (me_gz * ZP).astype(F32)
    nz = float(ngz * ZP)

    def wrapped(value, period):
        value = jnp.where(value >= period / 2, value - period, value)
        return jnp.where(value < -period / 2, value + period, value)

    turned = jnp.transpose(jnp.concatenate([events, events], axis=0))
    ex = wrapped(turned[0:1] - x0, float(NX))
    ez = wrapped(turned[2:3] - z0, nz)
    cell = lax.broadcasted_iota(jnp.int32, (TILE, 128), 0)
    dx = ((cell >> 3) - 2).astype(F32) - ex
    dz = ((cell & 7) - 2).astype(F32) - ez
    room = 256.0 - dx * dx - dz * dz
    second = (lax.broadcasted_iota(jnp.int32, (1, 128), 1) >> 6).astype(F32)
    for t in range(REACH // 2):
        dy = second + float(2 * t)
        amat[:, 128 * t : 128 * t + 128] = jnp.maximum(room - dy * dy, 0.0).astype(BF16)

    en = events[:, 3:4]
    column = lax.broadcasted_iota(jnp.int32, (SLOTS, NY), 1).astype(F32)
    away = wrapped(column - events[:, 1:2], float(NY))
    distance = jnp.abs(away).astype(BF16)
    def wide(value):
        return jnp.where(column >= 0.0, value, 0.0)

    number = wide(en)
    factors = [
        number.astype(BF16),
        (number * wide(wrapped(events[:, 0:1] - x0, float(NX)))).astype(BF16),
        (number * away).astype(BF16),
        (number * wide(wrapped(events[:, 2:3] - z0, nz))).astype(BF16),
    ]
    nothing = jnp.zeros((SLOTS, NY), BF16)
    for step in range(REACH):
        match = distance == jnp.full((SLOTS, NY), step, BF16)
        for which, factor in enumerate(factors):
            bmat[step * SLOTS : (step + 1) * SLOTS, which * NY : (which + 1) * NY] = jnp.where(
                match, factor, nothing
            )

    def total(which):
        return jnp.dot(
            amat[...], bmat[:, which * NY : (which + 1) * NY], preferred_element_type=F32
        )

    here = lax.broadcasted_iota(jnp.int32, (TILE, NY), 0)
    mass = total(0)
    block = (XR + 4, 8, NY)
    src[0] = (mass * (1.0 / 256.0)).reshape(block)
    src[1] = ((((here >> 3) - 2).astype(F32) * mass - total(1)) * (1.0 / 2048.0)).reshape(block)
    src[2] = (total(2) * (1.0 / 2048.0)).reshape(block)
    src[3] = ((((here & 7) - 2).astype(F32) * mass - total(3)) * (1.0 / 2048.0)).reshape(block)

    for copy in local:
        copy.wait()
    for copy in halos[:first]:
        copy.wait_recv()

    def with_source(field, i):
        return u[field, i] + src[field, i]

    def inner(field, i):
        return u[field, i, 2:6] + src[field, i, 2:6]

    @pl.loop(2, XR + 2)
    def _(i):
        rho = with_source(0, i)
        new = (1.0 - 6.0 * DIFF) * rho
        new += DIFF * (with_source(0, i - 1) + with_source(0, i + 1))
        new += ring(with_source(3, i), rho, 0)
        own = new[2:6] + ring(inner(2, i), rho[2:6], 1)
        own += A * (inner(1, i - 2) - inner(1, i + 2))
        own += (8.0 * A) * (inner(1, i + 1) - inner(1, i - 1))
        nd[i - 2] = own

    high, low = split(nd[...].reshape(XR * ZP, NY))
    both = jnp.dot(jnp.concatenate([high, low], axis=0), hi[...], preferred_element_type=F32)
    rows = XR * ZP
    full = both[:rows] + both[rows:] + jnp.dot(high, lo[...], preferred_element_type=F32)
    for t in range(2 * NY // 128):
        rmat[t] = full[:, 128 * t : 128 * t + 128]

    group = lax.broadcasted_iota(jnp.int32, (XR, 128), 1) >> 4

    @pl.loop(0, NY // 128)
    def _(t):
        parts = []
        for z in range(ZP):
            for half in range(2):
                parts.append(rmat[half * (NY // 128) + t, pl.ds(z, XR, stride=ZP), :])
        for d in range(8):
            value = parts[d]
            for g in range(8):
                if g != d:
                    value = jnp.where(group == g, pltpu.roll(parts[g], (16 * (g - d)) % 128, 1), value)
            outbox[t * 8 + d] = value

    for peer in peer_ids:
        send(outbox.at[peer], inbox.at[me_xy], a2a_s, a2a_r, 0, {"xy": peer}).start()

    inbox[me_xy] = outbox[me_xy]

    for copy in halos[first:]:
        copy.wait_recv()

    @pl.loop(0, XR + 4)
    def _(i):
        rho = with_source(0, i)
        m = [with_source(1 + c, i) for c in range(3)]
        b = [u[4 + c, i] for c in range(3)]
        u[0, i] = rho
        for c in range(3):
            u[1 + c, i] = m[c]
        inverse = 1.0 / rho
        v = [m[c] * inverse for c in range(3)]
        pressure = rho + 0.5 * (b[0] * b[0] + b[1] * b[1] + b[2] * b[2])
        fx[0, i] = m[0] * v[0] - b[0] * b[0] + pressure
        fx[1, i] = m[1] * v[0] - b[1] * b[0]
        fx[2, i] = m[2] * v[0] - b[2] * b[0]
        fx[3, i] = v[0] * b[1] - b[0] * v[1]
        fx[4, i] = v[0] * b[2] - b[0] * v[2]

    @pl.loop(2, XR + 2)
    def _(i):
        rho = u[0, i]
        m = [u[1 + c, i] for c in range(3)]
        b = [u[4 + c, i] for c in range(3)]
        inverse = 1.0 / rho
        v = [m[c] * inverse for c in range(3)]
        pressure = rho + 0.5 * (b[0] * b[0] + b[1] * b[1] + b[2] * b[2])

        def flux(c, k):
            value = m[c] * v[k] - b[c] * b[k]
            return value + pressure if c == k else value

        def along_x(field, which):
            value = DIFF * (u[field, i - 1] + u[field, i + 1])
            if which is not None:
                value += A * (fx[which, i - 2] - fx[which, i + 2])
                value += (8.0 * A) * (fx[which, i + 1] - fx[which, i - 1])
            return value

        def spread(field, axis):
            size = field.shape[axis]
            return DIFF * (pltpu.roll(field, 1, axis) + pltpu.roll(field, size - 1, axis))

        def slope(offset):
            return pot[pl.ds(i + 6 + offset, 1), :]

        keep = 1.0 - 6.0 * DIFF
        for c in range(3):
            new = keep * m[c] + along_x(1 + c, c)
            new += ring(flux(c, 1), m[c], 1)
            new += ring(flux(c, 2), m[c], 0)
            if c == 0:
                pull = A * (slope(-2) - slope(2)) + (8.0 * A) * (slope(1) - slope(-1))
                new += rho * pull
            if c == 1:
                own = jnp.broadcast_to(slope(0), (8, NY))
                pull = A * (pltpu.roll(own, 2, 1) - pltpu.roll(own, NY - 2, 1))
                pull += (8.0 * A) * (pltpu.roll(own, NY - 1, 1) - pltpu.roll(own, 1, 1))
                new += rho * pull
            nmom[c, i - 2] = new[2:6]
        for c in range(3):
            new = keep * b[c] + along_x(4 + c, None if c == 0 else 2 + c)
            if c == 1:
                new += spread(b[c], 1)
            else:
                new += ring(v[1] * b[c] - b[1] * v[c], b[c], 1)
            if c == 2:
                new += spread(b[c], 0)
            else:
                new += ring(v[2] * b[c] - b[2] * v[c], b[c], 0)
            nmag[c, i - 2] = new[2:6]

    for copy in halos:
        copy.wait_send()
    drain(ev_s.at[0], ev.at[0 : len(slots)])
    drain(a2a_s.at[0], outbox.at[0 : nxy - 1])
    drain(a2a_r.at[0], inbox.at[0 : nxy - 1])

    high, low = split(inbox[...].reshape(NX, 128))

    def across(lhs, rhs):
        return lax.dot_general(
            lhs, rhs, (((0,), (0,)), ((), ())), preferred_element_type=F32
        )

    both = across(jnp.concatenate([high, low], axis=1), hi[...])
    full = both[:128] + both[128:] + across(high, lo[...])
    scale = 1.0 / 512.0
    wave_y = lax.broadcasted_iota(jnp.int32, (16, NX), 0) + me_xy * 16
    wave_x = lax.broadcasted_iota(jnp.int32, (16, NX), 1)
    origin = (wave_y == 0) & (wave_x == 0)
    for z in range(ZP):
        re = full[32 * z : 32 * z + 16]
        im = full[32 * z + 16 : 32 * z + 32]
        modes[0, z] = jnp.where(origin, 0.0, (re[:, :NX] - im[:, NX:]) * scale)
        modes[1, z] = jnp.where(origin, 0.0, (re[:, NX:] + im[:, :NX]) * -scale)


def deliver(*refs):
    count = (len(refs) - 1) // 2
    sems = refs[-1]
    copies = [
        pltpu.make_async_copy(refs[i], refs[count + i], sems.at[i]) for i in range(count)
    ]
    for copy in copies:
        copy.start()
    for copy in copies:
        copy.wait()


def on_device(nxy, ngz, high, low, density, momentum, magnetic, arm_potential, sn_cells, sn_counts):
    hbm = pl.BlockSpec(memory_space=pl.ANY)
    smem = pl.BlockSpec(memory_space=pltpu.SMEM)
    halo = 18

    def body(*refs):
        kernel(nxy, ngz, *refs)

    dma = pltpu.SemaphoreType.DMA
    shapes = ((XR, ZP, NY), (3, XR, ZP, NY), (3, XR, ZP, NY), (2, ZP, 16, NX))
    results = pl.pallas_call(
        body,
        out_shape=tuple(pltpu.VMEM(shape, F32) for shape in shapes),
        in_specs=[hbm, hbm, hbm, hbm, smem, smem, hbm, hbm],
        out_specs=tuple(pl.BlockSpec(memory_space=pltpu.VMEM) for _ in shapes),
        scratch_shapes=[
            pltpu.VMEM((7, XR + 4, 8, NY), F32),
            pltpu.VMEM((4, XR + 4, 8, NY), F32),
            pltpu.VMEM((5, XR + 4, 8, NY), F32),
            pltpu.VMEM((32, NY), F32),
            pltpu.VMEM((SLOTS, 1, 128), F32),
            pltpu.VMEM((TILE, REACH * SLOTS), BF16),
            pltpu.VMEM((REACH * SLOTS, 4 * NY), BF16),
            pltpu.VMEM((NY, 2 * NY), BF16),
            pltpu.VMEM((NY, 2 * NY), BF16),
            pltpu.VMEM((2 * NY // 128, XR * ZP, 128), F32),
            pltpu.VMEM((nxy, XR, 128), F32),
            pltpu.VMEM((nxy, XR, 128), F32),
            dma((6,)),
            dma((1,)), dma((1,)),
            dma((halo,)), dma((halo,)),
            dma((1,)), dma((1,)),
        ],
        compiler_params=pltpu.CompilerParams(collective_id=0, has_side_effects=True),
    )(density, momentum, magnetic, arm_potential, sn_cells, sn_counts, high, low)
    return pl.pallas_call(
        deliver,
        out_shape=tuple(jax.ShapeDtypeStruct(shape, F32) for shape in shapes),
        in_specs=[hbm] * 4,
        out_specs=(hbm,) * 4,
        scratch_shapes=[dma((4,))],
        compiler_params=pltpu.CompilerParams(vmem_limit_bytes=16 * 1024 * 1024),
    )(*results)


def solution(mesh):
    nxy, ngz = mesh.shape["xy"], mesh.shape["gz"]
    high, low = tables()

    def step(*arrays):
        return on_device(nxy, ngz, jnp.asarray(high), jnp.asarray(low), *arrays)

    in_specs = (
        P("xy", "gz", None),
        P(None, "xy", "gz", None),
        P(None, "xy", "gz", None),
        P("xy", None),
        P(("gz", "xy"), None),
        P(("gz", "xy")),
    )
    out_specs = (
        P("xy", "gz", None),
        P(None, "xy", "gz", None),
        P(None, "xy", "gz", None),
        P(None, "gz", "xy", None),
    )
    return jax.shard_map(step, mesh=mesh, in_specs=in_specs, out_specs=out_specs, check_vma=False)
```

```python
import jax
import jax.numpy as jnp
import ml_dtypes
import numpy as np
from jax import lax
from jax.experimental import pallas as pl
from jax.experimental.pallas import tpu as pltpu
from jax.sharding import PartitionSpec as P

MESH = pl.DeviceIdType.MESH
F32 = jnp.float32
BF16 = jnp.bfloat16

NX, NY = 512, 512
XR, ZP = 16, 4
RX, RZ = 5, 11
SLOTS = 64
REACH = 16
TORUS_X = 4
A = -0.1 / 12.0
DIFF = 0.05
TILE = (XR + 4) * 8


def tables():
    wave = np.arange(NY)
    angle = (wave[:, None] * wave[None, :] % NY) * (2.0 * np.pi / NY)
    full = np.concatenate([np.cos(angle), np.sin(angle)], axis=1)
    high = full.astype(ml_dtypes.bfloat16)
    low = (full - high.astype(np.float64)).astype(ml_dtypes.bfloat16)
    return high, low


def split(value):
    high = value.astype(BF16)
    return high, (value - high.astype(F32)).astype(BF16)


def ring(flux, field, axis):
    size = flux.shape[axis]
    near = DIFF * field
    steep = (8.0 * A) * flux
    far = A * flux
    return (
        pltpu.roll(near - steep, 1, axis)
        + pltpu.roll(near + steep, size - 1, axis)
        + pltpu.roll(far, 2, axis)
        - pltpu.roll(far, size - 2, axis)
    )


def kernel(
    nxy, ngz,
    rho_ref, mom_ref, mag_ref, pot_ref, cells_ref, counts_ref, hi_ref, lo_ref,
    nd, nmom, nmag, modes,
    u, src, fx, pot, ev, amat, bmat, hi, lo, rmat, outbox, inbox, cells, counts,
    local_sem, ev_s, ev_r, halo_s, halo_r, a2a_s, a2a_r,
):
    me_xy = lax.axis_index("xy")
    me_gz = lax.axis_index("gz")

    def shifted(me, k, size):
        there = me + k
        if k < 0:
            return jnp.where(there < 0, there + size, there)
        return jnp.where(there >= size, there - size, there)

    row_of = {k: shifted(me_xy, k, nxy) for k in range(-(nxy // 2), nxy - nxy // 2)}
    plane_of = {k: shifted(me_gz, k, ngz) for k in range(-(RZ // 2), RZ // 2 + 1)}
    peers = sorted((k for k in row_of if k), key=lambda k: (-abs(k), k))

    ny = nxy // TORUS_X
    me_y = me_xy // TORUS_X
    me_x = me_xy - TORUS_X * me_y
    y_order = [ny // 2] + [sign * k for k in range(ny // 2 - 1, 0, -1) for sign in (-1, 1)] + [0]
    peer_ids = [
        shifted(me_y, dy, ny) * TORUS_X + shifted(me_x, dx, TORUS_X)
        for dx in (2, 1, 3, 0)
        for dy in y_order
        if dx or dy
    ]

    fetch = [
        pltpu.make_async_copy(cells_ref, cells, local_sem.at[6]),
        pltpu.make_async_copy(counts_ref, counts, local_sem.at[7]),
    ]
    for copy in fetch:
        copy.start()

    barrier = pltpu.get_barrier_semaphore()
    middle = (RX * RZ) // 2
    slots = [slot for slot in range(RX * RZ) if slot != middle]

    def owner(slot):
        return {"xy": row_of[slot // RZ - RX // 2], "gz": plane_of[slot % RZ - RZ // 2]}

    beyond = [k for k in peers if abs(k) > RX // 2]
    for slot in slots:
        pl.semaphore_signal(barrier, inc=1, device_id=owner(slot), device_id_type=MESH)
    for k in beyond:
        pl.semaphore_signal(barrier, inc=1, device_id={"xy": row_of[k]}, device_id_type=MESH)

    local = [
        pltpu.make_async_copy(rho_ref, u.at[0, 2:18, 2:6], local_sem.at[0]),
        pltpu.make_async_copy(mom_ref, u.at[1:4, 2:18, 2:6], local_sem.at[1]),
        pltpu.make_async_copy(mag_ref, u.at[4:7, 2:18, 2:6], local_sem.at[2]),
        pltpu.make_async_copy(pot_ref, pot.at[8:24], local_sem.at[3]),
        pltpu.make_async_copy(hi_ref, hi, local_sem.at[4]),
        pltpu.make_async_copy(lo_ref, lo, local_sem.at[5]),
    ]
    for copy in local:
        copy.start()

    for copy in fetch:
        copy.wait()
    lane = lax.broadcasted_iota(jnp.int32, (1, 128), 1)
    row = jnp.where(lane == 0, cells[0, 0], 0)
    row = jnp.where(lane == 1, cells[0, 1], row)
    row = jnp.where(lane == 2, cells[0, 2], row)
    row = jnp.where(lane == 3, counts[0], row)
    ev[middle] = row.astype(F32)
    for slot in range(RX * RZ, SLOTS):
        ev[slot] = jnp.zeros((1, 128), F32)

    pl.semaphore_wait(barrier, len(slots) + len(beyond))

    def send(source, target, sems, recvs, index, where):
        return pltpu.make_async_remote_copy(
            src_ref=source, dst_ref=target, send_sem=sems.at[index], recv_sem=recvs.at[index],
            device_id=where, device_id_type=MESH,
        )

    def drain(sem, ref):
        pltpu.make_async_copy(ref, ref, sem).wait()

    def event(slot):
        return send(ev.at[middle], ev.at[slot], ev_s, ev_r, 0, owner(RX * RZ - 1 - slot))

    for slot in slots:
        event(slot).start()

    up, down = {"xy": row_of[1]}, {"xy": row_of[-1]}
    above, below = {"gz": plane_of[1]}, {"gz": plane_of[-1]}
    low_x, high_x = slice(0, 2), slice(18, 20)
    low_z, high_z = slice(0, 2), slice(6, 8)
    own_x, own_z = slice(2, 18), slice(2, 6)
    pairs = [
        (rho_ref.at[:, 2:4], u.at[0, own_x, low_z], above),
        (rho_ref.at[:, 0:2], u.at[0, own_x, high_z], below),
        (mom_ref.at[2, :, 2:4], u.at[3, own_x, low_z], above),
        (mom_ref.at[2, :, 0:2], u.at[3, own_x, high_z], below),
        (rho_ref.at[14:16], u.at[0, low_x, own_z], up),
        (rho_ref.at[0:2], u.at[0, high_x, own_z], down),
        (mom_ref.at[0, 14:16], u.at[1, low_x, own_z], up),
        (mom_ref.at[0, 0:2], u.at[1, high_x, own_z], down),
        (mom_ref.at[0:2, :, 2:4], u.at[1:3, own_x, low_z], above),
        (mom_ref.at[0:2, :, 0:2], u.at[1:3, own_x, high_z], below),
        (mag_ref.at[:, :, 2:4], u.at[4:7, own_x, low_z], above),
        (mag_ref.at[:, :, 0:2], u.at[4:7, own_x, high_z], below),
        (mom_ref.at[1:3, 14:16], u.at[2:4, low_x, own_z], up),
        (mom_ref.at[1:3, 0:2], u.at[2:4, high_x, own_z], down),
        (mag_ref.at[:, 14:16], u.at[4:7, low_x, own_z], up),
        (mag_ref.at[:, 0:2], u.at[4:7, high_x, own_z], down),
        (pot_ref.at[14:16], pot.at[6:8], up),
        (pot_ref.at[0:2], pot.at[24:26], down),
    ]
    halos = [send(s, t, halo_s, halo_r, index, w) for index, (s, t, w) in enumerate(pairs)]
    first = 8
    for copy in halos[:first]:
        copy.start()

    for copy in halos[first:]:
        copy.start()

    drain(ev_r.at[0], ev.at[0 : len(slots)])

    events = ev[...].reshape(SLOTS, 128)
    x0 = (me_xy * XR).astype(F32)
    z0 = (me_gz * ZP).astype(F32)
    nz = float(ngz * ZP)

    def wrapped(value, period):
        value = jnp.where(value >= period / 2, value - period, value)
        return jnp.where(value < -period / 2, value + period, value)

    turned = jnp.transpose(jnp.concatenate([events, events], axis=0))
    ex = wrapped(turned[0:1] - x0, float(NX))
    ez = wrapped(turned[2:3] - z0, nz)
    cell = lax.broadcasted_iota(jnp.int32, (TILE, 128), 0)
    dx = ((cell >> 3) - 2).astype(F32) - ex
    dz = ((cell & 7) - 2).astype(F32) - ez
    room = 256.0 - dx * dx - dz * dz
    second = (lax.broadcasted_iota(jnp.int32, (1, 128), 1) >> 6).astype(F32)
    for t in range(REACH // 2):
        dy = second + float(2 * t)
        amat[:, 128 * t : 128 * t + 128] = jnp.maximum(room - dy * dy, 0.0).astype(BF16)

    en = events[:, 3:4]
    column = lax.broadcasted_iota(jnp.int32, (SLOTS, NY), 1).astype(F32)
    away = wrapped(column - events[:, 1:2], float(NY))
    distance = jnp.abs(away).astype(BF16)
    def wide(value):
        return jnp.where(column >= 0.0, value, 0.0)

    number = wide(en)
    factors = [
        number.astype(BF16),
        (number * wide(wrapped(events[:, 0:1] - x0, float(NX)))).astype(BF16),
        (number * away).astype(BF16),
        (number * wide(wrapped(events[:, 2:3] - z0, nz))).astype(BF16),
    ]
    nothing = jnp.zeros((SLOTS, NY), BF16)
    for step in range(REACH):
        match = distance == jnp.full((SLOTS, NY), step, BF16)
        for which, factor in enumerate(factors):
            bmat[step * SLOTS : (step + 1) * SLOTS, which * NY : (which + 1) * NY] = jnp.where(
                match, factor, nothing
            )

    def total(which):
        return jnp.dot(
            amat[...], bmat[:, which * NY : (which + 1) * NY], preferred_element_type=F32
        )

    here = lax.broadcasted_iota(jnp.int32, (TILE, NY), 0)
    mass = total(0)
    block = (XR + 4, 8, NY)
    src[0] = (mass * (1.0 / 256.0)).reshape(block)
    src[1] = ((((here >> 3) - 2).astype(F32) * mass - total(1)) * (1.0 / 2048.0)).reshape(block)
    src[2] = (total(2) * (1.0 / 2048.0)).reshape(block)
    src[3] = ((((here & 7) - 2).astype(F32) * mass - total(3)) * (1.0 / 2048.0)).reshape(block)

    for copy in local:
        copy.wait()
    for copy in halos[:first]:
        copy.wait_recv()

    def with_source(field, i):
        return u[field, i] + src[field, i]

    def inner(field, i):
        return u[field, i, 2:6] + src[field, i, 2:6]

    @pl.loop(2, XR + 2)
    def _(i):
        rho = with_source(0, i)
        new = (1.0 - 6.0 * DIFF) * rho
        new += DIFF * (with_source(0, i - 1) + with_source(0, i + 1))
        new += ring(with_source(3, i), rho, 0)
        own = new[2:6] + ring(inner(2, i), rho[2:6], 1)
        own += A * (inner(1, i - 2) - inner(1, i + 2))
        own += (8.0 * A) * (inner(1, i + 1) - inner(1, i - 1))
        nd[i - 2] = own

    high, low = split(nd[...].reshape(XR * ZP, NY))
    both = jnp.dot(jnp.concatenate([high, low], axis=0), hi[...], preferred_element_type=F32)
    rows = XR * ZP
    full = both[:rows] + both[rows:] + jnp.dot(high, lo[...], preferred_element_type=F32)
    for t in range(2 * NY // 128):
        rmat[t] = full[:, 128 * t : 128 * t + 128]

    group = lax.broadcasted_iota(jnp.int32, (XR, 128), 1) >> 4

    @pl.loop(0, NY // 128)
    def _(t):
        parts = []
        for z in range(ZP):
            for half in range(2):
                parts.append(rmat[half * (NY // 128) + t, pl.ds(z, XR, stride=ZP), :])
        for d in range(8):
            value = parts[d]
            for g in range(8):
                if g != d:
                    value = jnp.where(group == g, pltpu.roll(parts[g], (16 * (g - d)) % 128, 1), value)
            outbox[t * 8 + d] = value

    for peer in peer_ids:
        send(outbox.at[peer], inbox.at[me_xy], a2a_s, a2a_r, 0, {"xy": peer}).start()

    inbox[me_xy] = outbox[me_xy]

    for copy in halos[first:]:
        copy.wait_recv()

    @pl.loop(0, XR + 4)
    def _(i):
        rho = with_source(0, i)
        m = [with_source(1 + c, i) for c in range(3)]
        b = [u[4 + c, i] for c in range(3)]
        u[0, i] = rho
        for c in range(3):
            u[1 + c, i] = m[c]
        inverse = 1.0 / rho
        v = [m[c] * inverse for c in range(3)]
        pressure = rho + 0.5 * (b[0] * b[0] + b[1] * b[1] + b[2] * b[2])
        fx[0, i] = m[0] * v[0] - b[0] * b[0] + pressure
        fx[1, i] = m[1] * v[0] - b[1] * b[0]
        fx[2, i] = m[2] * v[0] - b[2] * b[0]
        fx[3, i] = v[0] * b[1] - b[0] * v[1]
        fx[4, i] = v[0] * b[2] - b[0] * v[2]

    @pl.loop(2, XR + 2)
    def _(i):
        rho = u[0, i]
        m = [u[1 + c, i] for c in range(3)]
        b = [u[4 + c, i] for c in range(3)]
        inverse = 1.0 / rho
        v = [m[c] * inverse for c in range(3)]
        pressure = rho + 0.5 * (b[0] * b[0] + b[1] * b[1] + b[2] * b[2])

        def flux(c, k):
            value = m[c] * v[k] - b[c] * b[k]
            return value + pressure if c == k else value

        def along_x(field, which):
            value = DIFF * (u[field, i - 1] + u[field, i + 1])
            if which is not None:
                value += A * (fx[which, i - 2] - fx[which, i + 2])
                value += (8.0 * A) * (fx[which, i + 1] - fx[which, i - 1])
            return value

        def spread(field, axis):
            size = field.shape[axis]
            return DIFF * (pltpu.roll(field, 1, axis) + pltpu.roll(field, size - 1, axis))

        def slope(offset):
            return pot[pl.ds(i + 6 + offset, 1), :]

        keep = 1.0 - 6.0 * DIFF
        for c in range(3):
            new = keep * m[c] + along_x(1 + c, c)
            new += ring(flux(c, 1), m[c], 1)
            new += ring(flux(c, 2), m[c], 0)
            if c == 0:
                pull = A * (slope(-2) - slope(2)) + (8.0 * A) * (slope(1) - slope(-1))
                new += rho * pull
            if c == 1:
                own = jnp.broadcast_to(slope(0), (8, NY))
                pull = A * (pltpu.roll(own, 2, 1) - pltpu.roll(own, NY - 2, 1))
                pull += (8.0 * A) * (pltpu.roll(own, NY - 1, 1) - pltpu.roll(own, 1, 1))
                new += rho * pull
            nmom[c, i - 2] = new[2:6]
        for c in range(3):
            new = keep * b[c] + along_x(4 + c, None if c == 0 else 2 + c)
            if c == 1:
                new += spread(b[c], 1)
            else:
                new += ring(v[1] * b[c] - b[1] * v[c], b[c], 1)
            if c == 2:
                new += spread(b[c], 0)
            else:
                new += ring(v[2] * b[c] - b[2] * v[c], b[c], 0)
            nmag[c, i - 2] = new[2:6]

    for copy in halos:
        copy.wait_send()
    drain(ev_s.at[0], ev.at[0 : len(slots)])
    drain(a2a_s.at[0], outbox.at[0 : nxy - 1])
    drain(a2a_r.at[0], inbox.at[0 : nxy - 1])

    high, low = split(inbox[...].reshape(NX, 128))

    def across(lhs, rhs):
        return lax.dot_general(
            lhs, rhs, (((0,), (0,)), ((), ())), preferred_element_type=F32
        )

    both = across(jnp.concatenate([high, low], axis=1), hi[...])
    full = both[:128] + both[128:] + across(high, lo[...])
    scale = 1.0 / 512.0
    wave_y = lax.broadcasted_iota(jnp.int32, (16, NX), 0) + me_xy * 16
    wave_x = lax.broadcasted_iota(jnp.int32, (16, NX), 1)
    origin = (wave_y == 0) & (wave_x == 0)
    for z in range(ZP):
        re = full[32 * z : 32 * z + 16]
        im = full[32 * z + 16 : 32 * z + 32]
        modes[0, z] = jnp.where(origin, 0.0, (re[:, :NX] - im[:, NX:]) * scale)
        modes[1, z] = jnp.where(origin, 0.0, (re[:, NX:] + im[:, :NX]) * -scale)


def deliver(*refs):
    count = (len(refs) - 1) // 2
    sems = refs[-1]
    copies = [
        pltpu.make_async_copy(refs[i], refs[count + i], sems.at[i]) for i in range(count)
    ]
    for copy in copies:
        copy.start()
    for copy in copies:
        copy.wait()


def on_device(nxy, ngz, high, low, density, momentum, magnetic, arm_potential, sn_cells, sn_counts):
    hbm = pl.BlockSpec(memory_space=pl.ANY)
    halo = 18

    def body(*refs):
        kernel(nxy, ngz, *refs)

    dma = pltpu.SemaphoreType.DMA
    shapes = ((XR, ZP, NY), (3, XR, ZP, NY), (3, XR, ZP, NY), (2, ZP, 16, NX))
    results = pl.pallas_call(
        body,
        out_shape=tuple(pltpu.VMEM(shape, F32) for shape in shapes),
        in_specs=[hbm] * 8,
        out_specs=tuple(pl.BlockSpec(memory_space=pltpu.VMEM) for _ in shapes),
        scratch_shapes=[
            pltpu.VMEM((7, XR + 4, 8, NY), F32),
            pltpu.VMEM((4, XR + 4, 8, NY), F32),
            pltpu.VMEM((5, XR + 4, 8, NY), F32),
            pltpu.VMEM((32, NY), F32),
            pltpu.VMEM((SLOTS, 1, 128), F32),
            pltpu.VMEM((TILE, REACH * SLOTS), BF16),
            pltpu.VMEM((REACH * SLOTS, 4 * NY), BF16),
            pltpu.VMEM((NY, 2 * NY), BF16),
            pltpu.VMEM((NY, 2 * NY), BF16),
            pltpu.VMEM((2 * NY // 128, XR * ZP, 128), F32),
            pltpu.VMEM((nxy, XR, 128), F32),
            pltpu.VMEM((nxy, XR, 128), F32),
            pltpu.SMEM((1, 3), jnp.int32),
            pltpu.SMEM((1,), jnp.int32),
            dma((8,)),
            dma((1,)), dma((1,)),
            dma((halo,)), dma((halo,)),
            dma((1,)), dma((1,)),
        ],
        compiler_params=pltpu.CompilerParams(collective_id=0, has_side_effects=True),
    )(density, momentum, magnetic, arm_potential, sn_cells, sn_counts, high, low)
    return pl.pallas_call(
        deliver,
        out_shape=tuple(jax.ShapeDtypeStruct(shape, F32) for shape in shapes),
        in_specs=[hbm] * 4,
        out_specs=(hbm,) * 4,
        scratch_shapes=[dma((4,))],
        compiler_params=pltpu.CompilerParams(vmem_limit_bytes=16 * 1024 * 1024),
    )(*results)


def solution(mesh):
    nxy, ngz = mesh.shape["xy"], mesh.shape["gz"]
    high, low = tables()

    def step(*arrays):
        return on_device(nxy, ngz, jnp.asarray(high), jnp.asarray(low), *arrays)

    in_specs = (
        P("xy", "gz", None),
        P(None, "xy", "gz", None),
        P(None, "xy", "gz", None),
        P("xy", None),
        P(("gz", "xy"), None),
        P(("gz", "xy")),
    )
    out_specs = (
        P("xy", "gz", None),
        P(None, "xy", "gz", None),
        P(None, "xy", "gz", None),
        P(None, "gz", "xy", None),
    )
    return jax.shard_map(step, mesh=mesh, in_specs=in_specs, out_specs=out_specs, check_vma=False)
```

```python
import functools

import jax
import jax.numpy as jnp
import ml_dtypes
import numpy as np
from jax import lax
from jax.experimental import pallas as pl
from jax.experimental.pallas import tpu as pltpu
from jax.sharding import PartitionSpec as P

MESH = pl.DeviceIdType.MESH
F32 = jnp.float32
BF16 = jnp.bfloat16

NX, NY = 512, 512
XR, ZP = 16, 4
RX, RZ = 5, 11
SLOTS = 64
REACH = 16
A = -0.1 / 12.0
DIFF = 0.05
TILE = (XR + 4) * 8


def tables():
    wave = np.arange(NY)
    angle = (wave[:, None] * wave[None, :] % NY) * (2.0 * np.pi / NY)
    full = np.concatenate([np.cos(angle), np.sin(angle)], axis=1)
    high = full.astype(ml_dtypes.bfloat16)
    low = (full - high.astype(np.float64)).astype(ml_dtypes.bfloat16)
    return high, low


def split(value):
    high = value.astype(BF16)
    return high, (value - high.astype(F32)).astype(BF16)


def ring(flux, field, axis):
    size = flux.shape[axis]
    near = DIFF * field
    steep = (8.0 * A) * flux
    far = A * flux
    return (
        pltpu.roll(near - steep, 1, axis)
        + pltpu.roll(near + steep, size - 1, axis)
        + pltpu.roll(far, 2, axis)
        - pltpu.roll(far, size - 2, axis)
    )


def kernel(
    nxy, ngz,
    rho_ref, mom_ref, mag_ref, pot_ref, cells_ref, counts_ref, hi_ref, lo_ref,
    nd, nmom, nmag, modes,
    u, src, fx, pot, ev, amat, bmat, hi, lo, rmat, outbox, inbox, cells, counts,
    local_sem, ev_s, ev_r, halo_s, halo_r, a2a_s, a2a_r,
):
    me_xy = lax.axis_index("xy")
    me_gz = lax.axis_index("gz")

    def shifted(me, k, size):
        there = me + k
        if k < 0:
            return jnp.where(there < 0, there + size, there)
        return jnp.where(there >= size, there - size, there)

    row_of = {k: shifted(me_xy, k, nxy) for k in range(-(nxy // 2), nxy - nxy // 2)}
    plane_of = {k: shifted(me_gz, k, ngz) for k in range(-(RZ // 2), RZ // 2 + 1)}
    peers = sorted((k for k in row_of if k), key=lambda k: (-abs(k), k))

    fetch = [
        pltpu.make_async_copy(cells_ref, cells, local_sem.at[6]),
        pltpu.make_async_copy(counts_ref, counts, local_sem.at[7]),
    ]
    for copy in fetch:
        copy.start()

    barrier = pltpu.get_barrier_semaphore()
    middle = (RX * RZ) // 2
    slots = [slot for slot in range(RX * RZ) if slot != middle]

    def owner(slot):
        return {"xy": row_of[slot // RZ - RX // 2], "gz": plane_of[slot % RZ - RZ // 2]}

    beyond = [k for k in peers if abs(k) > RX // 2]
    for slot in slots:
        pl.semaphore_signal(barrier, inc=1, device_id=owner(slot), device_id_type=MESH)
    for k in beyond:
        pl.semaphore_signal(barrier, inc=1, device_id={"xy": row_of[k]}, device_id_type=MESH)

    local = [
        pltpu.make_async_copy(rho_ref, u.at[0, 2:18, 2:6], local_sem.at[0]),
        pltpu.make_async_copy(mom_ref, u.at[1:4, 2:18, 2:6], local_sem.at[1]),
        pltpu.make_async_copy(mag_ref, u.at[4:7, 2:18, 2:6], local_sem.at[2]),
        pltpu.make_async_copy(pot_ref, pot.at[8:24], local_sem.at[3]),
        pltpu.make_async_copy(hi_ref, hi, local_sem.at[4]),
        pltpu.make_async_copy(lo_ref, lo, local_sem.at[5]),
    ]
    for copy in local:
        copy.start()

    for copy in fetch:
        copy.wait()
    lane = lax.broadcasted_iota(jnp.int32, (1, 128), 1)
    row = jnp.where(lane == 0, cells[0, 0], 0)
    row = jnp.where(lane == 1, cells[0, 1], row)
    row = jnp.where(lane == 2, cells[0, 2], row)
    row = jnp.where(lane == 3, counts[0], row)
    ev[middle] = row.astype(F32)
    for slot in range(RX * RZ, SLOTS):
        ev[slot] = jnp.zeros((1, 128), F32)

    pl.semaphore_wait(barrier, len(slots) + len(beyond))

    def send(source, target, sems, recvs, index, where):
        return pltpu.make_async_remote_copy(
            src_ref=source, dst_ref=target, send_sem=sems.at[index], recv_sem=recvs.at[index],
            device_id=where, device_id_type=MESH,
        )

    def drain(sem, ref):
        pltpu.make_async_copy(ref, ref, sem).wait()

    def event(slot):
        return send(ev.at[middle], ev.at[slot], ev_s, ev_r, 0, owner(RX * RZ - 1 - slot))

    for slot in slots:
        event(slot).start()

    up, down = {"xy": row_of[1]}, {"xy": row_of[-1]}
    above, below = {"gz": plane_of[1]}, {"gz": plane_of[-1]}
    low_x, high_x = slice(0, 2), slice(18, 20)
    low_z, high_z = slice(0, 2), slice(6, 8)
    own_x, own_z = slice(2, 18), slice(2, 6)
    pairs = [
        (rho_ref.at[:, 2:4], u.at[0, own_x, low_z], above),
        (rho_ref.at[:, 0:2], u.at[0, own_x, high_z], below),
        (mom_ref.at[2, :, 2:4], u.at[3, own_x, low_z], above),
        (mom_ref.at[2, :, 0:2], u.at[3, own_x, high_z], below),
        (rho_ref.at[14:16], u.at[0, low_x, own_z], up),
        (rho_ref.at[0:2], u.at[0, high_x, own_z], down),
        (mom_ref.at[0, 14:16], u.at[1, low_x, own_z], up),
        (mom_ref.at[0, 0:2], u.at[1, high_x, own_z], down),
        (mom_ref.at[0:2, :, 2:4], u.at[1:3, own_x, low_z], above),
        (mom_ref.at[0:2, :, 0:2], u.at[1:3, own_x, high_z], below),
        (mag_ref.at[:, :, 2:4], u.at[4:7, own_x, low_z], above),
        (mag_ref.at[:, :, 0:2], u.at[4:7, own_x, high_z], below),
        (mom_ref.at[1:3, 14:16], u.at[2:4, low_x, own_z], up),
        (mom_ref.at[1:3, 0:2], u.at[2:4, high_x, own_z], down),
        (mag_ref.at[:, 14:16], u.at[4:7, low_x, own_z], up),
        (mag_ref.at[:, 0:2], u.at[4:7, high_x, own_z], down),
        (pot_ref.at[14:16], pot.at[6:8], up),
        (pot_ref.at[0:2], pot.at[24:26], down),
    ]
    halos = [send(s, t, halo_s, halo_r, index, w) for index, (s, t, w) in enumerate(pairs)]
    first = 8
    for copy in halos[:first]:
        copy.start()

    for copy in halos[first:]:
        copy.start()

    drain(ev_r.at[0], ev.at[0 : len(slots)])

    events = ev[...].reshape(SLOTS, 128)
    x0 = (me_xy * XR).astype(F32)
    z0 = (me_gz * ZP).astype(F32)
    nz = float(ngz * ZP)

    def wrapped(value, period):
        value = jnp.where(value >= period / 2, value - period, value)
        return jnp.where(value < -period / 2, value + period, value)

    turned = jnp.transpose(jnp.concatenate([events, events], axis=0))
    ex = wrapped(turned[0:1] - x0, float(NX))
    ez = wrapped(turned[2:3] - z0, nz)
    cell = lax.broadcasted_iota(jnp.int32, (TILE, 128), 0)
    dx = ((cell >> 3) - 2).astype(F32) - ex
    dz = ((cell & 7) - 2).astype(F32) - ez
    room = 256.0 - dx * dx - dz * dz
    second = (lax.broadcasted_iota(jnp.int32, (1, 128), 1) >> 6).astype(F32)
    for t in range(REACH // 2):
        dy = second + float(2 * t)
        amat[:, 128 * t : 128 * t + 128] = jnp.maximum(room - dy * dy, 0.0).astype(BF16)

    en = events[:, 3:4]
    column = lax.broadcasted_iota(jnp.int32, (SLOTS, NY), 1).astype(F32)
    away = wrapped(column - events[:, 1:2], float(NY))
    distance = jnp.abs(away).astype(BF16)
    def wide(value):
        return jnp.where(column >= 0.0, value, 0.0)

    number = wide(en)
    factors = [
        number.astype(BF16),
        (number * wide(wrapped(events[:, 0:1] - x0, float(NX)))).astype(BF16),
        (number * away).astype(BF16),
        (number * wide(wrapped(events[:, 2:3] - z0, nz))).astype(BF16),
    ]
    nothing = jnp.zeros((SLOTS, NY), BF16)
    for step in range(REACH):
        match = distance == jnp.full((SLOTS, NY), step, BF16)
        for which, factor in enumerate(factors):
            bmat[step * SLOTS : (step + 1) * SLOTS, which * NY : (which + 1) * NY] = jnp.where(
                match, factor, nothing
            )

    def total(which):
        return jnp.dot(
            amat[...], bmat[:, which * NY : (which + 1) * NY], preferred_element_type=F32
        )

    here = lax.broadcasted_iota(jnp.int32, (TILE, NY), 0)
    mass = total(0)
    block = (XR + 4, 8, NY)
    src[0] = (mass * (1.0 / 256.0)).reshape(block)
    src[1] = ((((here >> 3) - 2).astype(F32) * mass - total(1)) * (1.0 / 2048.0)).reshape(block)
    src[2] = (total(2) * (1.0 / 2048.0)).reshape(block)
    src[3] = ((((here & 7) - 2).astype(F32) * mass - total(3)) * (1.0 / 2048.0)).reshape(block)

    for copy in local:
        copy.wait()
    for copy in halos[:first]:
        copy.wait_recv()

    def with_source(field, i):
        return u[field, i] + src[field, i]

    def inner(field, i):
        return u[field, i, 2:6] + src[field, i, 2:6]

    @pl.loop(2, XR + 2)
    def _(i):
        rho = with_source(0, i)
        new = (1.0 - 6.0 * DIFF) * rho
        new += DIFF * (with_source(0, i - 1) + with_source(0, i + 1))
        new += ring(with_source(3, i), rho, 0)
        own = new[2:6] + ring(inner(2, i), rho[2:6], 1)
        own += A * (inner(1, i - 2) - inner(1, i + 2))
        own += (8.0 * A) * (inner(1, i + 1) - inner(1, i - 1))
        nd[i - 2] = own

    high, low = split(nd[...].reshape(XR * ZP, NY))
    both = jnp.dot(jnp.concatenate([high, low], axis=0), hi[...], preferred_element_type=F32)
    rows = XR * ZP
    full = both[:rows] + both[rows:] + jnp.dot(high, lo[...], preferred_element_type=F32)
    for t in range(2 * NY // 128):
        rmat[t] = full[:, 128 * t : 128 * t + 128]

    group = lax.broadcasted_iota(jnp.int32, (XR, 128), 1) >> 4

    def sort(t):
        parts = []
        for z in range(ZP):
            for half in range(2):
                parts.append(rmat[half * (NY // 128) + t, pl.ds(z, XR, stride=ZP), :])
        for d in range(8):
            value = parts[d]
            for g in range(8):
                if g != d:
                    value = jnp.where(group == g, pltpu.roll(parts[g], (16 * (g - d)) % 128, 1), value)
            outbox[t * 8 + d] = value

    def post(peer):
        send(outbox.at[peer], inbox.at[me_xy], a2a_s, a2a_r, 0, {"xy": peer}).start()

    eights = nxy // 8
    my_eight = me_xy // 8
    for away_by in [3, 1, 2, 0]:
        t = shifted(my_eight, away_by, eights)
        sort(t)
        for d in range(8):
            peer = t * 8 + d
            if away_by:
                post(peer)
            else:
                pl.when(peer != me_xy)(functools.partial(post, peer))

    inbox[me_xy] = outbox[me_xy]

    for copy in halos[first:]:
        copy.wait_recv()

    @pl.loop(0, XR + 4)
    def _(i):
        rho = with_source(0, i)
        m = [with_source(1 + c, i) for c in range(3)]
        b = [u[4 + c, i] for c in range(3)]
        u[0, i] = rho
        for c in range(3):
            u[1 + c, i] = m[c]
        inverse = 1.0 / rho
        v = [m[c] * inverse for c in range(3)]
        pressure = rho + 0.5 * (b[0] * b[0] + b[1] * b[1] + b[2] * b[2])
        fx[0, i] = m[0] * v[0] - b[0] * b[0] + pressure
        fx[1, i] = m[1] * v[0] - b[1] * b[0]
        fx[2, i] = m[2] * v[0] - b[2] * b[0]
        fx[3, i] = v[0] * b[1] - b[0] * v[1]
        fx[4, i] = v[0] * b[2] - b[0] * v[2]

    @pl.loop(2, XR + 2)
    def _(i):
        rho = u[0, i]
        m = [u[1 + c, i] for c in range(3)]
        b = [u[4 + c, i] for c in range(3)]
        inverse = 1.0 / rho
        v = [m[c] * inverse for c in range(3)]
        pressure = rho + 0.5 * (b[0] * b[0] + b[1] * b[1] + b[2] * b[2])

        def flux(c, k):
            value = m[c] * v[k] - b[c] * b[k]
            return value + pressure if c == k else value

        def along_x(field, which):
            value = DIFF * (u[field, i - 1] + u[field, i + 1])
            if which is not None:
                value += A * (fx[which, i - 2] - fx[which, i + 2])
                value += (8.0 * A) * (fx[which, i + 1] - fx[which, i - 1])
            return value

        def spread(field, axis):
            size = field.shape[axis]
            return DIFF * (pltpu.roll(field, 1, axis) + pltpu.roll(field, size - 1, axis))

        def slope(offset):
            return pot[pl.ds(i + 6 + offset, 1), :]

        keep = 1.0 - 6.0 * DIFF
        for c in range(3):
            new = keep * m[c] + along_x(1 + c, c)
            new += ring(flux(c, 1), m[c], 1)
            new += ring(flux(c, 2), m[c], 0)
            if c == 0:
                pull = A * (slope(-2) - slope(2)) + (8.0 * A) * (slope(1) - slope(-1))
                new += rho * pull
            if c == 1:
                own = jnp.broadcast_to(slope(0), (8, NY))
                pull = A * (pltpu.roll(own, 2, 1) - pltpu.roll(own, NY - 2, 1))
                pull += (8.0 * A) * (pltpu.roll(own, NY - 1, 1) - pltpu.roll(own, 1, 1))
                new += rho * pull
            nmom[c, i - 2] = new[2:6]
        for c in range(3):
            new = keep * b[c] + along_x(4 + c, None if c == 0 else 2 + c)
            if c == 1:
                new += spread(b[c], 1)
            else:
                new += ring(v[1] * b[c] - b[1] * v[c], b[c], 1)
            if c == 2:
                new += spread(b[c], 0)
            else:
                new += ring(v[2] * b[c] - b[2] * v[c], b[c], 0)
            nmag[c, i - 2] = new[2:6]

    for copy in halos:
        copy.wait_send()
    drain(ev_s.at[0], ev.at[0 : len(slots)])
    drain(a2a_s.at[0], outbox.at[0 : nxy - 1])
    drain(a2a_r.at[0], inbox.at[0 : nxy - 1])

    high, low = split(inbox[...].reshape(NX, 128))

    def across(lhs, rhs):
        return lax.dot_general(
            lhs, rhs, (((0,), (0,)), ((), ())), preferred_element_type=F32
        )

    both = across(jnp.concatenate([high, low], axis=1), hi[...])
    full = both[:128] + both[128:] + across(high, lo[...])
    scale = 1.0 / 512.0
    wave_y = lax.broadcasted_iota(jnp.int32, (16, NX), 0) + me_xy * 16
    wave_x = lax.broadcasted_iota(jnp.int32, (16, NX), 1)
    origin = (wave_y == 0) & (wave_x == 0)
    for z in range(ZP):
        re = full[32 * z : 32 * z + 16]
        im = full[32 * z + 16 : 32 * z + 32]
        modes[0, z] = jnp.where(origin, 0.0, (re[:, :NX] - im[:, NX:]) * scale)
        modes[1, z] = jnp.where(origin, 0.0, (re[:, NX:] + im[:, :NX]) * -scale)


def deliver(*refs):
    count = (len(refs) - 1) // 2
    sems = refs[-1]
    copies = [
        pltpu.make_async_copy(refs[i], refs[count + i], sems.at[i]) for i in range(count)
    ]
    for copy in copies:
        copy.start()
    for copy in copies:
        copy.wait()


def on_device(nxy, ngz, high, low, density, momentum, magnetic, arm_potential, sn_cells, sn_counts):
    hbm = pl.BlockSpec(memory_space=pl.ANY)
    halo = 18

    def body(*refs):
        kernel(nxy, ngz, *refs)

    dma = pltpu.SemaphoreType.DMA
    shapes = ((XR, ZP, NY), (3, XR, ZP, NY), (3, XR, ZP, NY), (2, ZP, 16, NX))
    results = pl.pallas_call(
        body,
        out_shape=tuple(pltpu.VMEM(shape, F32) for shape in shapes),
        in_specs=[hbm] * 8,
        out_specs=tuple(pl.BlockSpec(memory_space=pltpu.VMEM) for _ in shapes),
        scratch_shapes=[
            pltpu.VMEM((7, XR + 4, 8, NY), F32),
            pltpu.VMEM((4, XR + 4, 8, NY), F32),
            pltpu.VMEM((5, XR + 4, 8, NY), F32),
            pltpu.VMEM((32, NY), F32),
            pltpu.VMEM((SLOTS, 1, 128), F32),
            pltpu.VMEM((TILE, REACH * SLOTS), BF16),
            pltpu.VMEM((REACH * SLOTS, 4 * NY), BF16),
            pltpu.VMEM((NY, 2 * NY), BF16),
            pltpu.VMEM((NY, 2 * NY), BF16),
            pltpu.VMEM((2 * NY // 128, XR * ZP, 128), F32),
            pltpu.VMEM((nxy, XR, 128), F32),
            pltpu.VMEM((nxy, XR, 128), F32),
            pltpu.SMEM((1, 3), jnp.int32),
            pltpu.SMEM((1,), jnp.int32),
            dma((8,)),
            dma((1,)), dma((1,)),
            dma((halo,)), dma((halo,)),
            dma((1,)), dma((1,)),
        ],
        compiler_params=pltpu.CompilerParams(collective_id=0, has_side_effects=True),
    )(density, momentum, magnetic, arm_potential, sn_cells, sn_counts, high, low)
    return pl.pallas_call(
        deliver,
        out_shape=tuple(jax.ShapeDtypeStruct(shape, F32) for shape in shapes),
        in_specs=[hbm] * 4,
        out_specs=(hbm,) * 4,
        scratch_shapes=[dma((4,))],
        compiler_params=pltpu.CompilerParams(vmem_limit_bytes=16 * 1024 * 1024),
    )(*results)


def solution(mesh):
    nxy, ngz = mesh.shape["xy"], mesh.shape["gz"]
    high, low = tables()

    def step(*arrays):
        return on_device(nxy, ngz, jnp.asarray(high), jnp.asarray(low), *arrays)

    in_specs = (
        P("xy", "gz", None),
        P(None, "xy", "gz", None),
        P(None, "xy", "gz", None),
        P("xy", None),
        P(("gz", "xy"), None),
        P(("gz", "xy")),
    )
    out_specs = (
        P("xy", "gz", None),
        P(None, "xy", "gz", None),
        P(None, "xy", "gz", None),
        P(None, "gz", "xy", None),
    )
    return jax.shard_map(step, mesh=mesh, in_specs=in_specs, out_specs=out_specs, check_vma=False)
```
